256 devices in a mesh: col: 32 (over z, x), row: 8 (over y, core).
Axes of the slice: x: 4, y: 4, z: 8, core: 2. Of those that a mesh axis runs over, the one named last changes fastest.
Arguments:
- trailing: float32 [24576, 16384], P('row', 'col'), may hold values from -6 to 6
- panel_rows: float32 [24576, 512], P(('row', 'col')), may hold values from -6 to 6
- pivot_block: float32 [512, 512], P('col'), as said below
- panel_fill: int32 [96, 2], replicated, may hold values 0 or 1
Outputs:
- updated: float32 [24576, 16384], P('row', 'col')
- panel_factor: float32 [24576, 512], P(('row', 'col'))
The draws below stay inside these ranges and needn't reach their ends.
Inputs may be any that keep to these rules, and one draw needn't show every extreme that they name: `pivot_block`: Symmetric; each diagonal entry exceeds the sum of the magnitudes of the other entries of its row by at least 1. `panel_fill`: each entry is 1 with probability 0.15, independently of the others.
All inputs are finite; a program needn't handle non-finite values.
Results may differ from the reference program's by a relative error of at most 0.00008.
Values sent between devices are 32-bit elements; how exact they have to be, the bound alone decides.
A program may use at most 128 MiB of HBM per device.

```python
import jax
import jax.numpy as jnp
from jax import lax

B = 256
NR = 96
NC = 64


def draw_pivot_block(key, part):
    pivot_order = 2 * B
    first_key, second_key = jax.random.split(jax.random.fold_in(key, 17))
    spread = 8.0
    diag_extra = jax.random.uniform(second_key, (pivot_order,), jnp.float32, 1.0, 2.0)
    magnitudes = jax.random.uniform(first_key, (pivot_order, pivot_order), jnp.float32, 0.6, 1.0) * (spread / pivot_order)
    upper_part = jnp.triu(magnitudes, 1)
    coupling = -(upper_part + upper_part.T)
    identity = jnp.eye(pivot_order, dtype=jnp.float32)
    return coupling + identity * (spread + diag_extra)[None, :]


def set_ends(array, key, least, high):
    index_at = [jax.random.randint(jax.random.fold_in(key, axis), (), 0, length) for axis, length in enumerate(array.shape)]
    main_axis = array.shape.index(max(array.shape))
    next_to = index_at[:main_axis] + [(index_at[main_axis] + 1) % array.shape[main_axis]] + index_at[main_axis + 1:]
    return array.at[tuple(index_at)].set(least).at[tuple(next_to)].set(high)


def block_scale(rng, shape, shards, low, top_value):
    gain, own = 1.0, jax.random.fold_in(rng, 6)
    for dim, shards_of in shards:
        steps = jnp.exp(jax.random.uniform(jax.random.fold_in(own, dim), (shards_of,), jnp.float32, low / len(shards), top_value / len(shards)))
        gain = gain * jnp.repeat(steps, shape[dim] // shards_of).reshape([-1 if axis == dim else 1 for axis in range(len(shape))])
    return gain


def noise(stream_key, dims, scale, reach, shards=(), kind=jnp.bfloat16):
    drawn = jax.random.normal(stream_key, dims, jnp.float32) * scale
    if len(shards) > 0:
        drawn = block_scale(stream_key, dims, shards, -0.22, 0.18) * drawn
    return jnp.clip(drawn, min=-reach, max=reach).astype(kind)


def setup_inputs(seed: int = 0) -> dict:
    arg_keys = jax.random.split(jax.random.key(seed), 5)
    trailing = noise(arg_keys[0], (NR * B, NC * B), 1.0, 6.0, ((0, 8), (1, 32)), jnp.float32)
    panel_rows = noise(arg_keys[1], (NR * B, 2 * B), 1.0, 6.0, ((0, 256),), jnp.float32)
    pivot_block = draw_pivot_block(jax.random.fold_in(arg_keys[4], 71), 0)
    panel_fill = set_ends((jax.random.randint(arg_keys[3], (NR, 2), 0, 20) < 3).astype(jnp.int32), jax.random.fold_in(arg_keys[3], 1), 0, 1)
    return {"trailing": trailing, "panel_rows": panel_rows, "pivot_block": pivot_block, "panel_fill": panel_fill}


def reference(trailing, panel_rows, pivot_block, panel_fill):
    flags = jnp.repeat(panel_fill.astype(jnp.float32), B, axis=0)
    total_rows = panel_rows.shape[0]
    masked = (panel_rows.reshape(total_rows, 2, B) * flags[:, :, None]).reshape(total_rows, 2 * B)
    factor = jnp.linalg.cholesky(pivot_block)
    panel_factor = lax.linalg.triangular_solve(factor, masked, left_side=False, lower=True, transpose_a=True)
    columns = panel_factor[:trailing.shape[1]]
    update = lax.dot_general(panel_factor, columns, (((1,), (1,)), ((), ())), precision=lax.Precision.HIGHEST)
    updated = trailing - update
    return (updated, panel_factor)
```

```python
import functools

import jax
import jax.numpy as jnp
from jax import lax
from jax.experimental import pallas as pl
from jax.experimental.pallas import tpu as pltpu
from jax.sharding import PartitionSpec as P

F32 = jnp.float32
BF16 = jnp.bfloat16
HIGHEST = lax.Precision.HIGHEST
NT = (((1,), (1,)), ((), ()))
NN = (((1,), (0,)), ((), ()))
TN = (((0,), (0,)), ((), ()))

ZS, XS = 8, 4
COLS, ROWS = ZS * XS, 8
B = 256
TILE = 128


def mm(a, b, dims):
    return lax.dot_general(a, b, dims, precision=HIGHEST, preferred_element_type=F32)


def split(v):
    hi = v.astype(BF16)
    return hi, (v - hi.astype(F32)).astype(BF16)


def mm3(a, b, dims):
    dot = functools.partial(lax.dot_general, dimension_numbers=dims, preferred_element_type=F32)
    return dot(a[0], b[0]) + (dot(a[0], b[1]) + dot(a[1], b[0]))


def spread_row(v, r):
    return jnp.broadcast_to(v[r : r + 1, :], v.shape)


def invert_tile(groups, hook):
    n = groups[0].shape[1]
    count = n // 8
    lane = lax.broadcasted_iota(jnp.int32, (8, n), 1)
    sub = lax.broadcasted_iota(jnp.int32, (8, n), 0)
    left = list(groups)
    right = [jnp.where(lane == sub + 8 * g, 1.0, 0.0).astype(F32) for g in range(count)]
    done = []

    def columns(h, g):
        return [
            jnp.broadcast_to(left[h][:, 8 * g + r : 8 * g + r + 1], (8, n)) for r in range(8)
        ]

    def total(terms):
        while len(terms) > 1:
            terms = [a + b for a, b in zip(terms[::2], terms[1::2])]
        return terms[0]

    for g in range(count):
        hook(g)
        pivot = columns(g, g)
        below = {h: columns(h, g) for h in range(g + 1, count)}
        wide, inv = left[g], right[g]
        final = inv
        for r in range(0, 8, 2):
            a, b, d = (
                spread_row(pivot[r], r),
                spread_row(pivot[r + 1], r),
                spread_row(pivot[r + 1], r + 1),
            )
            det = a * d - b * b
            scale = 1.0 / det
            an, bn, dn = a * scale, b * scale, d * scale
            m0, m1 = pivot[r], pivot[r + 1]
            e0, e1 = spread_row(inv, r), spread_row(inv, r + 1)
            over_a = 1.0 / a
            f0 = e0 * lax.rsqrt(a)
            f1 = (e1 - (b * over_a) * e0) * lax.rsqrt(det * over_a)
            final = jnp.where(sub == r, f0, jnp.where(sub == r + 1, f1, final))

            def step(w):
                w0, w1 = spread_row(w, r), spread_row(w, r + 1)
                y0 = dn * w0 - bn * w1
                y1 = an * w1 - bn * w0
                rest = w - (m0 * y0 + m1 * y1)
                return jnp.where(sub == r, y0, jnp.where(sub == r + 1, y1, rest))

            for q in range(r + 2, 8):
                pivot[q] = step(pivot[q])
            wide, inv = step(wide), step(inv)
        done.append(final)
        wide_rows = [spread_row(wide, r) for r in range(8)]
        inv_rows = [spread_row(inv, r) for r in range(8)]
        for h in range(g + 1, count):
            left[h] = left[h] - total([below[h][r] * wide_rows[r] for r in range(8)])
            right[h] = right[h] - total([below[h][r] * inv_rows[r] for r in range(8)])
    return done


def gather_kernel(slots, fill, pivot, panel, z_out, mc, slab, work, full, staged, queued, packed,
                  piv_send, piv_recv, ex_send, ex_recv, q_send, q_recv, c_send, c_recv,
                  x_send, x_recv, x_own, r_send, r_recv, y_send, y_recv, k_send, k_recv):
    col, row = lax.axis_index("col"), lax.axis_index("row")
    zi, xi = col // XS, col % XS
    y, core = row // 2, row % 2
    halves = queued.shape[0]
    per = halves // 2

    def remote(src, dst, send, recv, c, r):
        return pltpu.make_async_remote_copy(
            src_ref=src, dst_ref=dst, send_sem=send, recv_sem=recv,
            device_id={"col": c, "row": r}, device_id_type=pl.DeviceIdType.MESH)

    def local(src, dst, sem):
        return pltpu.make_async_copy(src, dst, sem)

    def send_pivot(i, _):
        remote(pivot.at[core], full.at[col, core], piv_send, piv_recv.at[col // 8],
               (col + i) % COLS, row).start()
        return 0

    local(pivot.at[core], full.at[col, core], piv_recv.at[col // 8]).start()
    lax.fori_loop(1, COLS, send_pivot, 0)

    for t in range(per):
        for h in range(2):
            staged[t, h] = panel[8 * t : 8 * t + 8, B * h : B * h + B]

    def send_group(t, _):
        index = per * col + t
        target, block = index % COLS, index // COLS

        @pl.when(target != col)
        def _():
            remote(staged.at[t], queued.at[pl.ds(2 * block, 2)], q_send, q_recv, target, row).start()

        @pl.when(target == col)
        def _():
            local(staged.at[t], queued.at[pl.ds(2 * block, 2)], q_recv).start()
        return 0

    def send_column(t, _):
        index = per * col + t
        target_col = 6 * row + index // 64
        target_row = index % 8
        place = (index % 64) // 8
        own = jnp.logical_and(target_col == col, target_row == row)

        @pl.when(jnp.logical_and(target_col < COLS, jnp.logical_not(own)))
        def _():
            remote(staged.at[t], mc.at[place, target_row], c_send, c_recv, target_col, target_row).start()

        @pl.when(own)
        def _():
            local(staged.at[t], mc.at[place, target_row], c_recv).start()
        return 0

    lax.fori_loop(0, per, send_group, 0)
    lax.fori_loop(0, per, send_column, 0)

    if slots < halves:
        base = per * row
        where = [jnp.int32(0)] * slots
        seen = jnp.int32(0)
        for n in range(halves):
            flag = fill[2 * (base + n // 2) + n % 2]
            for k in range(slots):
                hit = jnp.logical_and(flag != 0, seen == k)
                where[k] = jnp.where(hit, n, where[k])
            seen = seen + jnp.where(flag != 0, 1, 0)
    else:
        where = list(range(slots))

    def exchange(q):
        part = full.at[pl.ds(8 * q, 8), core]
        return remote(part, part, ex_send.at[q], ex_recv.at[q], col, y * 2 + 1 - core)

    for q in range(4):
        part = full.at[pl.ds(8 * q, 8), core]
        local(part, part, piv_recv.at[q]).wait()
        exchange(q).start()

    def wait_exchange(q):
        exchange(q).wait_recv()

    def pack():
        local(queued, queued, q_recv).wait()
        for k in range(slots):
            packed[k] = queued[where[k]]
        local(packed, slab.at[:, col], x_own).start()
        for dx in range(1, XS):
            remote(packed, slab.at[:, col], x_send.at[dx - 1], x_recv.at[dx - 1],
                   zi * XS + (xi + dx) % XS, row).start()

    def column_y():
        part = mc.at[:, row]
        local(part, part, c_recv).wait()
        for dy in range(1, 4):
            remote(part, part, y_send.at[dy - 1], y_recv.at[dy - 1], col, ((y + dy) % 4) * 2 + core).start()

    def core_part(i):
        part = mc.at[:, 2 * ((y + i) % 4) + core]
        return remote(part, part, k_send.at[i], k_recv.at[i], col, y * 2 + 1 - core)

    def column_core():
        for dy in range(1, 4):
            part = mc.at[:, row]
            remote(part, part, y_send.at[dy - 1], y_recv.at[dy - 1], col, ((y + dy) % 4) * 2 + core).wait_recv()
        for i in range(4):
            core_part(i).start()

    def ring(step, side):
        sign = 1 if side == 0 else -1
        source = (zi - sign * step + ZS) % ZS
        if step < 3:
            part = slab.at[:, pl.ds(XS * source, XS)]
        else:
            part = slab.at[pl.ds(side * (slots // 2), slots // 2), pl.ds(XS * source, XS)]
        target = ((zi + sign + ZS) % ZS) * XS + xi
        return remote(part, part, r_send.at[side, step], r_recv.at[side, step], target, row)

    def ring_first():
        local(packed, slab.at[:, col], x_own).wait()
        for dx in range(1, XS):
            remote(packed, slab.at[:, col], x_send.at[dx - 1], x_recv.at[dx - 1],
                   zi * XS + (xi + dx) % XS, row).wait_recv()
        for side in range(2):
            ring(0, side).start()

    def ring_next(step):
        for side in range(2):
            ring(step - 1, side).wait_recv()
            ring(step, side).start()

    plan = {
        (0, 3): pack,
        (0, 5): column_y,
        (0, 13): ring_first,
        (1, 3): column_core,
        (1, 8): functools.partial(ring_next, 1),
        (2, 6): functools.partial(ring_next, 2),
        (3, 4): functools.partial(ring_next, 3),
    }

    n = z_out.shape[0]
    z_out[...] = jnp.zeros_like(z_out)
    wait_exchange(0)
    for k in range(n // TILE):
        lo, hi = k * TILE, (k + 1) * TILE
        if k == 0:
            groups = [full[g // 2, g % 2, :, lo:hi] for g in range(TILE // 8)]
        else:
            groups = [work[lo + 8 * g : lo + 8 * g + 8, lo:hi] for g in range(TILE // 8)]

        def hook(g, k=k):
            if (k, g) in plan:
                plan[k, g]()

        rows = invert_tile(groups, hook)
        for g in range(TILE // 8):
            z_out[lo + 8 * g : lo + 8 * g + 8, lo:hi] = rows[g]
        zk = z_out[lo:hi, lo:hi]
        if k > 0:
            z_out[lo:hi, :lo] = mm(zk, z_out[lo:hi, :lo], NN)
        if hi < n:
            if k == 0:
                for q in range(1, 4):
                    wait_exchange(q)
                below = full[hi // 16 :].reshape(n - hi, n)
                p = mm(below[:, lo:hi], zk, NT)
                work[hi:, hi:] = below[:, hi:] - mm(p, p, NT)
            else:
                p = mm(work[hi:, lo:hi], zk, NT)
                work[hi:, hi:] = work[hi:, hi:] - mm(p, p, NT)
            z_out[hi:, :hi] = z_out[hi:, :hi] - mm(p, z_out[lo:hi, :hi], NN)

    for side in range(2):
        ring(3, side).wait_recv()
    for i in range(4):
        core_part(i).wait_recv()
    for i in range(4):
        core_part(i).wait_send()
        exchange(i).wait_send()
    for side in range(2):
        for step in range(4):
            ring(step, side).wait_send()
    for dx in range(1, XS):
        remote(packed, slab.at[:, col], x_send.at[dx - 1], x_recv.at[dx - 1],
               zi * XS + (xi + dx) % XS, row).wait_send()
    for dy in range(1, 4):
        part = mc.at[:, row]
        remote(part, part, y_send.at[dy - 1], y_recv.at[dy - 1], col, ((y + dy) % 4) * 2 + core).wait_send()
    local(full.at[pl.ds(0, COLS - 1), core], full.at[pl.ds(0, COLS - 1), core], piv_send).wait()

    def sent_group(t, _):
        @pl.when((per * col + t) % COLS != col)
        def _():
            local(staged.at[0], staged.at[0], q_send).wait()
        return 0

    def sent_column(t, _):
        index = per * col + t
        target_col = 6 * row + index // 64
        own = jnp.logical_and(target_col == col, index % 8 == row)

        @pl.when(jnp.logical_and(target_col < COLS, jnp.logical_not(own)))
        def _():
            local(staged.at[0], staged.at[0], c_send).wait()
        return 0

    lax.fori_loop(0, per, sent_group, 0)
    lax.fori_loop(0, per, sent_column, 0)


def gather_and_factor(slots, fill, pivot, panel):
    n = panel.shape[1]
    per = panel.shape[0] // 8
    dma = pltpu.SemaphoreType.DMA
    vmem = pl.BlockSpec(memory_space=pltpu.VMEM)
    anywhere = pl.BlockSpec(memory_space=pl.ANY)
    return pl.pallas_call(
        functools.partial(gather_kernel, slots),
        out_shape=(
            jax.ShapeDtypeStruct((n, n), F32),
            jax.ShapeDtypeStruct((8, ROWS, 2, 8, B), F32),
            jax.ShapeDtypeStruct((slots, COLS, 8, B), F32),
        ),
        in_specs=[pl.BlockSpec(memory_space=pltpu.SMEM), vmem, vmem],
        out_specs=(vmem, anywhere, anywhere),
        scratch_shapes=[
            pltpu.VMEM((n, n), F32),
            pltpu.VMEM((COLS, 2, 8, n), F32),
            pltpu.VMEM((per, 2, 8, B), F32),
            pltpu.VMEM((2 * per, 8, B), F32),
            pltpu.VMEM((slots, 8, B), F32),
            dma, dma((4,)), dma((4,)), dma((4,)),
            dma, dma, dma, dma,
            dma((3,)), dma((3,)), dma,
            dma((2, 4)), dma((2, 4)), dma((3,)), dma((3,)), dma((4,)), dma((4,)),
        ],
        compiler_params=pltpu.CompilerParams(has_side_effects=True, vmem_limit_bytes=40 << 20),
        name="gather_and_factor",
    )(fill, pivot.reshape(2, 8, n), panel)


def update_kernel(slots, fill, z, mc, slab, panel, trailing, updated, own, blocks, t_hi, t_lo,
                  mc_v, slab_v, read_sem, write_sem, mc_sem, slab_sem):
    col, row = lax.axis_index("col"), lax.axis_index("row")
    count = blocks.shape[0]
    base = count * row

    def read(b):
        return pltpu.make_async_copy(trailing.at[pl.ds(B * b, B)], blocks.at[b], read_sem.at[b])

    def write(b):
        return pltpu.make_async_copy(blocks.at[b], updated.at[pl.ds(B * b, B)], write_sem.at[b])

    get_mc = pltpu.make_async_copy(mc, mc_v, mc_sem)
    get_slab = pltpu.make_async_copy(slab, slab_v, slab_sem)
    get_mc.start()
    get_slab.start()
    for b in range(count):
        read(b).start()

    def flag(block, h):
        return jnp.where(fill[2 * block + h] != 0, 1.0, 0.0).astype(F32)

    zv = z[...]
    zs = split(zv)
    masked = []
    for t in range(panel.shape[0] // 8):
        block = base + (panel.shape[0] * col + 8 * t) // B
        masked.append(jnp.concatenate(
            [panel[8 * t : 8 * t + 8, B * h : B * h + B] * flag(block, h) for h in range(2)], axis=1))
    own[...] = mm(jnp.concatenate(masked, axis=0), zv, NT)

    get_mc.wait()
    rows = []
    for i in range(2):
        part = mc_v[4 * i : 4 * i + 4]
        rows.append(jnp.concatenate(
            [part[:, :, h].reshape(B, B) * flag(2 * col + i, h) for h in range(2)], axis=1))
    xc = mm3(split(jnp.concatenate(rows, axis=0)), zs, NT)
    t_hi[...], t_lo[...] = split(mm3(zs, tuple(v.T for v in split(xc)), TN))
    get_slab.wait()

    seen = jnp.int32(0)
    for b in range(count):
        read(b).wait()
        for h in range(2):
            on = fill[2 * (base + b) + h] != 0
            slot = seen if slots < 2 * count else 2 * b + h

            @pl.when(on)
            def _(b=b, h=h, slot=slot):
                m = split(slab_v[slot].reshape(B, B))
                t = (t_hi[B * h : B * h + B], t_lo[B * h : B * h + B])
                blocks[b] = blocks[b] - mm3(m, t, NN)

            seen = seen + jnp.where(on, 1, 0)
        write(b).start()
    for b in range(count):
        write(b).wait()


def apply_update(slots, fill, z, mc, slab, panel, trailing):
    n = panel.shape[1]
    count = trailing.shape[0] // B
    width = trailing.shape[1]
    dma = pltpu.SemaphoreType.DMA
    vmem = pl.BlockSpec(memory_space=pltpu.VMEM)
    anywhere = pl.BlockSpec(memory_space=pl.ANY)
    return pl.pallas_call(
        functools.partial(update_kernel, slots),
        out_shape=(
            jax.ShapeDtypeStruct(trailing.shape, F32),
            jax.ShapeDtypeStruct(panel.shape, F32),
        ),
        in_specs=[pl.BlockSpec(memory_space=pltpu.SMEM), vmem, anywhere, anywhere, vmem, anywhere],
        out_specs=(anywhere, vmem),
        scratch_shapes=[
            pltpu.VMEM((count, B, width), F32),
            pltpu.VMEM((n, width), BF16),
            pltpu.VMEM((n, width), BF16),
            pltpu.VMEM(mc.shape, F32),
            pltpu.VMEM(slab.shape, F32),
            dma((count,)), dma((count,)), dma, dma,
        ],
        compiler_params=pltpu.CompilerParams(vmem_limit_bytes=48 << 20),
        name="apply_update",
    )(fill, z, mc, slab, panel, trailing)


def per_device(trailing, panel_rows, pivot_block, panel_fill):
    fill = panel_fill.reshape(-1)
    halves = 2 * (trailing.shape[0] // B)

    def path(slots):
        def run(trailing, panel, pivot, fill):
            z, mc, slab = gather_and_factor(slots, fill, pivot, panel)
            return apply_update(slots, fill, z, mc, slab, panel, trailing)

        return run

    most = jnp.max(jnp.sum((fill != 0).reshape(ROWS, halves).astype(jnp.int32), axis=1))
    return lax.cond(most <= 8, path(8), path(halves), trailing, panel_rows, pivot_block, fill)


def solution(mesh):
    in_specs = (P("row", "col"), P(("row", "col"), None), P("col", None), P())
    out_specs = (P("row", "col"), P(("row", "col"), None))
    return jax.shard_map(
        per_device, mesh=mesh, in_specs=in_specs, out_specs=out_specs, check_vma=False
    )
```

```python
import functools

import jax
import jax.numpy as jnp
from jax import lax
from jax.experimental import pallas as pl
from jax.experimental.pallas import tpu as pltpu
from jax.sharding import PartitionSpec as P

F32 = jnp.float32
BF16 = jnp.bfloat16
HIGHEST = lax.Precision.HIGHEST
NT = (((1,), (1,)), ((), ()))
NN = (((1,), (0,)), ((), ()))
TN = (((0,), (0,)), ((), ()))

ZS, XS = 8, 4
COLS, ROWS = ZS * XS, 8
B = 256
TILE = 128


def mm(a, b, dims):
    return lax.dot_general(a, b, dims, precision=HIGHEST, preferred_element_type=F32)


def split(v):
    hi = v.astype(BF16)
    return hi, (v - hi.astype(F32)).astype(BF16)


def mm3(a, b, dims):
    dot = functools.partial(lax.dot_general, dimension_numbers=dims, preferred_element_type=F32)
    return dot(a[0], b[0]) + (dot(a[0], b[1]) + dot(a[1], b[0]))


def spread_row(v, r):
    return jnp.broadcast_to(v[r : r + 1, :], v.shape)


def invert_tile(groups, hook):
    n = groups[0].shape[1]
    count = n // 8
    lane = lax.broadcasted_iota(jnp.int32, (8, n), 1)
    sub = lax.broadcasted_iota(jnp.int32, (8, n), 0)
    left = list(groups)
    right = [jnp.where(lane == sub + 8 * g, 1.0, 0.0).astype(F32) for g in range(count)]
    done = []

    def columns(h, g):
        return [
            jnp.broadcast_to(left[h][:, 8 * g + r : 8 * g + r + 1], (8, n)) for r in range(8)
        ]

    def total(terms):
        while len(terms) > 1:
            terms = [a + b for a, b in zip(terms[::2], terms[1::2])]
        return terms[0]

    for g in range(count):
        hook(g)
        pivot = columns(g, g)
        below = {h: columns(h, g) for h in range(g + 1, count)}
        wide, inv = left[g], right[g]
        final = inv
        for r in range(0, 8, 2):
            a, b, d = (
                spread_row(pivot[r], r),
                spread_row(pivot[r + 1], r),
                spread_row(pivot[r + 1], r + 1),
            )
            det = a * d - b * b
            scale = 1.0 / det
            an, bn, dn = a * scale, b * scale, d * scale
            m0, m1 = pivot[r], pivot[r + 1]
            e0, e1 = spread_row(inv, r), spread_row(inv, r + 1)
            over_a = 1.0 / a
            f0 = e0 * lax.rsqrt(a)
            f1 = (e1 - (b * over_a) * e0) * lax.rsqrt(det * over_a)
            final = jnp.where(sub == r, f0, jnp.where(sub == r + 1, f1, final))

            def step(w):
                w0, w1 = spread_row(w, r), spread_row(w, r + 1)
                y0 = dn * w0 - bn * w1
                y1 = an * w1 - bn * w0
                rest = w - (m0 * y0 + m1 * y1)
                return jnp.where(sub == r, y0, jnp.where(sub == r + 1, y1, rest))

            for q in range(r + 2, 8):
                pivot[q] = step(pivot[q])
            wide, inv = step(wide), step(inv)
        done.append(final)
        wide_rows = [spread_row(wide, r) for r in range(8)]
        inv_rows = [spread_row(inv, r) for r in range(8)]
        for h in range(g + 1, count):
            left[h] = left[h] - total([below[h][r] * wide_rows[r] for r in range(8)])
            right[h] = right[h] - total([below[h][r] * inv_rows[r] for r in range(8)])
    return done

SLOTS = 8


def remote(src, dst, send, recv, col, row):
    return pltpu.make_async_remote_copy(
        src_ref=src, dst_ref=dst, send_sem=send, recv_sem=recv,
        device_id={"col": col, "row": row}, device_id_type=pl.DeviceIdType.MESH)


local = pltpu.make_async_copy


def place():
    col, row = lax.axis_index("col"), lax.axis_index("row")
    return col, row, col // XS, col % XS, row // 2, row % 2


def slots_of(fill, base, first, slots, halves):
    where = [jnp.int32(0)] * slots
    seen = jnp.int32(0)
    for n in range(halves):
        on = fill[n % 2, base + n // 2] != 0
        for k in range(slots):
            hit = jnp.logical_and(on, seen == first + k)
            where[k] = jnp.where(hit, n, where[k])
        seen = seen + jnp.where(on, 1, 0)
    return where


class SlabGather:
    def __init__(self, staged, queued, packed, slab, q_send, q_recv, x_send, x_recv, x_own, r_send, r_recv):
        self.refs = staged, queued, packed, slab
        self.q_send, self.q_recv, self.x_own = q_send, q_recv, x_own
        self.x_send, self.x_recv, self.r_send, self.r_recv = x_send, x_recv, r_send, r_recv
        self.slots = packed.shape[0]
        self.per = staged.shape[0]

    def stage(self, panel):
        staged = self.refs[0]
        for t in range(self.per):
            for h in range(2):
                staged[t, h] = panel[8 * t : 8 * t + 8, B * h : B * h + B]

    def target(self, t):
        index = self.per * place()[0] + t
        return index // COLS, (index % ZS) * XS + (index % COLS) // ZS

    def spread(self):
        staged, queued, _, _ = self.refs
        col, row, *_ = place()

        def send(t, _):
            block, target = self.target(t)
            there = queued.at[pl.ds(2 * block, 2)]

            @pl.when(target != col)
            def _():
                remote(staged.at[t], there, self.q_send, self.q_recv, target, row).start()

            @pl.when(target == col)
            def _():
                local(staged.at[t], there, self.q_recv).start()
            return 0

        lax.fori_loop(0, self.per, send, 0)

    def along_x(self, dx):
        _, _, packed, slab = self.refs
        col, row, zi, xi, *_ = place()
        half = self.slots // 2
        return remote(packed.at[pl.ds(0, half)], slab.at[pl.ds(0, half), zi, xi],
                      self.x_send.at[dx - 1], self.x_recv.at[dx - 1], zi * XS + (xi + dx) % XS, row)

    def across_x(self, z, start, count, dx):
        slab = self.refs[3]
        col, row, zi, xi, *_ = place()
        part = slab.at[pl.ds(start, count), z, xi]
        return remote(part, part, self.x_send.at[dx + 2], self.x_recv.at[dx + 2],
                      zi * XS + (xi + dx) % XS, row)

    def pass_across(self, z):
        half = self.slots // 2
        for dx in range(1, XS):
            self.across_x(z, half, half, dx).start()

    def own(self):
        _, _, packed, slab = self.refs
        _, _, zi, xi, *_ = place()
        return local(packed, slab.at[:, zi, xi], self.x_own)

    def pack(self, where):
        _, queued, packed, _ = self.refs
        zi = place()[2]
        local(queued, queued, self.q_recv).wait()
        for k in range(self.slots):
            packed[k] = queued[where[k]]
        self.own().start()
        for dx in range(1, XS):
            self.along_x(dx).start()
        self.own().wait()
        for side in range(2):
            self.ring(1, 0, side).start()
        self.pass_across(zi)

    def source(self, step, side):
        sign = 1 if side == 0 else -1
        return (place()[2] - sign * step + ZS) % ZS

    def ring(self, kind, step, side):
        slab = self.refs[3]
        col, row, zi, xi, *_ = place()
        sign = 1 if side == 0 else -1
        half = self.slots // 2
        rows = pl.ds(kind * half, half) if step < 3 else pl.ds(kind * half + side * (half // 2), half // 2)
        part = slab.at[rows, self.source(step, side)] if kind == 0 else slab.at[rows, self.source(step, side), xi]
        target = ((zi + sign + ZS) % ZS) * XS + xi
        return remote(part, part, self.r_send.at[kind, side, step], self.r_recv.at[kind, side, step], target, row)

    def first(self):
        for dx in range(1, XS):
            self.along_x(dx).wait_recv()
        for side in range(2):
            self.ring(0, 0, side).start()
        self.next_across(1)

    def next_across(self, step):
        for side in range(2):
            self.ring(1, step - 1, side).wait_recv()
            if step < 4:
                self.ring(1, step, side).start()
        if step < 4:
            for side in range(2):
                self.pass_across(self.source(step, side))
        else:
            self.pass_across(self.source(4, 0))

    def next(self, step):
        for side in range(2):
            self.ring(0, step - 1, side).wait_recv()
            self.ring(0, step, side).start()
        self.next_across(step + 1)

    def last(self):
        staged, _, _, slab = self.refs
        half = self.slots // 2
        col = place()[0]
        for side in range(2):
            self.ring(0, 3, side).wait_recv()
        line = slab.at[pl.ds(half, half), :, 0]
        for dx in range(1, XS):
            local(line, line, self.x_recv.at[dx + 2]).wait()
            local(line, line, self.x_send.at[dx + 2]).wait()
            self.along_x(dx).wait_send()
        for kind in range(2):
            for side in range(2):
                for step in range(4):
                    self.ring(kind, step, side).wait_send()

        def sent(t, _):
            @pl.when(self.target(t)[1] != col)
            def _():
                local(staged.at[0], staged.at[0], self.q_send).wait()
            return 0

        lax.fori_loop(0, self.per, sent, 0)


def slab_scratch(per, slots):
    dma = pltpu.SemaphoreType.DMA
    return [
        pltpu.VMEM((per, 2, 8, B), F32), pltpu.VMEM((2 * per, 8, B), F32), pltpu.VMEM((slots, 8, B), F32),
        dma, dma, dma((6,)), dma((6,)), dma, dma((2, 2, 4)), dma((2, 2, 4)),
    ]


def gather_kernel(fill_any, pivot_any, panel_any, trailing, z_out, t_hi, t_lo, slab, held, fill, pivot, panel, work, full, mc,
                  in_sem, held_sem, zs_send, zs_recv, zx_send, zx_recv, ex_send, ex_recv, c_send, c_recv,
                  y_send, y_recv, k_send, k_recv, staged, queued, packed, *slab_sems):
    col, row, zi, xi, y, core = place()
    halves = queued.shape[0]
    per = staged.shape[0]
    blocks = halves // 2
    gather = SlabGather(staged, queued, packed, slab, *slab_sems)
    loads = [
        local(fill_any, fill, in_sem.at[0]),
        local(pivot_any, pivot, in_sem.at[1]),
        local(panel_any, panel, in_sem.at[2]),
    ]
    for load in loads:
        load.start()

    def column_target(t):
        index = per * col + t
        target_col, target_row = 6 * row + index // 64, index % 8
        own = jnp.logical_and(target_col == col, target_row == row)
        return (index % 64) // 8, target_col, target_row, own

    def column_sends(t):
        _, target_col, _, own = column_target(t)
        return jnp.logical_and(target_col < COLS, jnp.logical_not(own))

    barrier = pltpu.get_barrier_semaphore()

    def greet(c, r):
        pl.semaphore_signal(barrier, inc=1, device_id={"col": c, "row": r}, device_id_type=pl.DeviceIdType.MESH)

    def greet_slab(i, _):
        greet((col + i) % COLS, row)
        return 0

    lax.fori_loop(1, COLS, greet_slab, 0)
    greet(col, 2 * y + 1 - core)
    for dy in range(1, 4):
        greet(col, 2 * ((y + dy) % 4) + core)

    def greet_column(s, _):
        source = (64 * (col % 6) + 8 * s + row) // per
        source_row = col // 6

        @pl.when(jnp.logical_not(jnp.logical_and(source == col, source_row == row)))
        def _():
            greet(source, source_row)
        return 0

    lax.fori_loop(0, 8, greet_column, 0)
    expected = jnp.int32(COLS - 1 + 4)
    for t in range(per):
        expected = expected + jnp.where(column_sends(t), 1, 0)
    z_out[...] = jnp.zeros_like(z_out)
    for load in loads:
        load.wait()
    gather.stage(panel)
    pl.semaphore_wait(barrier, expected)

    def pivot_z(dz):
        target = ((zi + dz) % ZS) * XS + xi
        return remote(pivot.at[core], full.at[zi, xi, core], zs_send, zs_recv.at[zi], target, row)

    def pivot_from(z):
        part = full.at[z, xi, core]
        return local(part, part, zs_recv.at[z])

    def pivot_x(part, dx):
        rows = full.at[pl.ds(0, 2), xi, core] if part == 0 else full.at[pl.ds(2, ZS - 2), xi, core]
        return remote(rows, rows, zx_send.at[part, dx - 1], zx_recv.at[part, dx - 1],
                      zi * XS + (xi + dx) % XS, row)

    def exchange(part):
        rows = full.at[pl.ds(0, 2), :, core] if part == 0 else full.at[pl.ds(2, ZS - 2), :, core]
        return remote(rows, rows, ex_send.at[part], ex_recv.at[part], col, 2 * y + 1 - core)

    local(pivot.at[core], full.at[zi, xi, core], zs_recv.at[zi]).start()
    for dz in (4, 3, 5, 2, 6, 1, 7):
        pivot_z(dz).start()
    gather.spread()

    def send_column(t, _):
        slot, target_col, target_row, own = column_target(t)
        there = mc.at[slot, target_row]

        @pl.when(column_sends(t))
        def _():
            remote(staged.at[t], there, c_send, c_recv, target_col, target_row).start()

        @pl.when(own)
        def _():
            local(staged.at[t], there, c_recv).start()
        return 0

    lax.fori_loop(0, per, send_column, 0)
    where = slots_of(fill, blocks * row, 0, SLOTS, halves)
    for z in range(2):
        pivot_from(z).wait()
    for dx in range(1, XS):
        pivot_x(0, dx).start()
    for z in range(2, ZS):
        pivot_from(z).wait()
    for dx in range(1, XS):
        pivot_x(1, dx).start()
    gather.pack(where)
    for dx in range(1, XS):
        pivot_x(0, dx).wait_recv()
    exchange(0).start()
    hold = local(trailing, held, held_sem)
    hold.start()

    def pivot_rest():
        for dx in range(1, XS):
            pivot_x(1, dx).wait_recv()
        exchange(1).start()

    def column_y(dy):
        part = mc.at[:, row]
        return remote(part, part, y_send.at[dy - 1], y_recv.at[dy - 1], col, 2 * ((y + dy) % 4) + core)

    def column_first():
        part = mc.at[:, row]
        local(part, part, c_recv).wait()
        for dy in range(1, 4):
            column_y(dy).start()

    def column_core(i):
        part = mc.at[:, 2 * i + core]
        return remote(part, part, k_send.at[i], k_recv.at[i], col, 2 * y + 1 - core)

    def column_next():
        for dy in range(1, 4):
            column_y(dy).wait_recv()
        for i in range(4):
            column_core(i).start()

    plan = {
        (0, 3): pivot_rest,
        (0, 4): gather.first,
        (0, 11): column_first,
        (1, 2): functools.partial(gather.next, 1),
        (1, 15): functools.partial(gather.next, 2),
        (2, 6): column_next,
        (2, 14): functools.partial(gather.next, 3),
    }

    n = z_out.shape[0]
    exchange(0).wait_recv()
    for k in range(n // TILE):
        lo, hi = k * TILE, (k + 1) * TILE
        if k == 0:
            groups = [full[g // 8, (g // 2) % 4, g % 2, :, lo:hi] for g in range(TILE // 8)]
        else:
            groups = [work[lo + 8 * g : lo + 8 * g + 8, lo:hi] for g in range(TILE // 8)]

        def hook(g, k=k):
            if (k, g) in plan:
                plan[k, g]()

        rows = invert_tile(groups, hook)
        for g in range(TILE // 8):
            z_out[lo + 8 * g : lo + 8 * g + 8, lo:hi] = rows[g]
        zk = z_out[lo:hi, lo:hi]
        if k > 0:
            z_out[lo:hi, :lo] = mm(zk, z_out[lo:hi, :lo], NN)
        if hi < n:
            if k == 0:
                exchange(1).wait_recv()
                below = full[2:].reshape(n - hi, n)
            else:
                below = work[hi:, :]
            p = mm(below[:, lo:hi], zk, NT)
            work[hi:, hi:] = below[:, hi:] - mm(p, p, NT)
            z_out[hi:, :hi] = z_out[hi:, :hi] - mm(p, z_out[lo:hi, :hi], NN)

    for i in range(4):
        column_core(i).wait_recv()

    def flag(block, h):
        return jnp.where(fill[h, block] != 0, 1.0, 0.0).astype(F32)

    rows = []
    for i in range(2):
        part = mc[4 * i : 4 * i + 4]
        rows.append(jnp.concatenate(
            [part[:, :, h].reshape(B, B) * flag(2 * col + i, h) for h in range(2)], axis=1))
    zs = split(z_out[...])
    xc = mm3(zs, split(jnp.concatenate(rows, axis=0)), NT)
    t_hi[...], t_lo[...] = split(mm3(zs, split(xc), TN))

    gather.last()
    hold.wait()
    for i in range(4):
        column_core(i).wait_send()
    for dy in range(1, 4):
        column_y(dy).wait_send()
    for part in range(2):
        exchange(part).wait_send()
        for dx in range(1, XS):
            pivot_x(part, dx).wait_send()
    local(full.at[pl.ds(0, ZS - 1), 0, core], full.at[pl.ds(0, ZS - 1), 0, core], zs_send).wait()

    def sent_column(t, _):
        @pl.when(column_sends(t))
        def _():
            local(staged.at[0], staged.at[0], c_send).wait()
        return 0

    lax.fori_loop(0, per, sent_column, 0)


def gather_and_factor(fill, pivot, panel, trailing):
    n = panel.shape[1]
    per = panel.shape[0] // 8
    dma = pltpu.SemaphoreType.DMA
    vmem = pl.BlockSpec(memory_space=pltpu.VMEM)
    anywhere = pl.BlockSpec(memory_space=pl.ANY)
    return pl.pallas_call(
        gather_kernel,
        out_shape=(
            jax.ShapeDtypeStruct((n, n), F32),
            jax.ShapeDtypeStruct((n, n), BF16),
            jax.ShapeDtypeStruct((n, n), BF16),
            jax.ShapeDtypeStruct((SLOTS, ZS, XS, 8, B), F32),
            jax.ShapeDtypeStruct(trailing.shape, F32),
        ),
        in_specs=[pl.BlockSpec(memory_space=pltpu.HBM)] * 4,
        out_specs=(vmem, vmem, vmem, anywhere, vmem),
        scratch_shapes=[
            pltpu.SMEM(fill.shape, jnp.int32),
            pltpu.VMEM((2, 8, n), F32),
            pltpu.VMEM(panel.shape, F32),
            pltpu.VMEM((n, n), F32),
            pltpu.VMEM((ZS, XS, 2, 8, n), F32),
            pltpu.VMEM((8, ROWS, 2, 8, B), F32),
            dma((3,)), dma, dma, dma((ZS,)), dma((2, 3)), dma((2, 3)), dma((2,)), dma((2,)), dma, dma,
            dma((3,)), dma((3,)), dma((4,)), dma((4,)),
        ] + slab_scratch(per, SLOTS),
        compiler_params=pltpu.CompilerParams(
            has_side_effects=True, collective_id=0, vmem_limit_bytes=30 << 20),
        name="gather_and_factor",
    )(fill, pivot.reshape(2, 8, n), panel, trailing)


def gather_more_kernel(first, fill, panel, slab, staged, queued, packed, *sems):
    row = lax.axis_index("row")
    halves = queued.shape[0]
    gather = SlabGather(staged, queued, packed, slab, *sems)
    gather.stage(panel)
    gather.spread()
    gather.pack(slots_of(fill, halves // 2 * row, first[0], SLOTS, halves))
    gather.first()
    for step in range(1, 4):
        gather.next(step)
    gather.last()


def gather_more(first, fill, panel):
    per = panel.shape[0] // 8
    smem = pl.BlockSpec(memory_space=pltpu.SMEM)
    return pl.pallas_call(
        gather_more_kernel,
        out_shape=jax.ShapeDtypeStruct((SLOTS, ZS, XS, 8, B), F32),
        in_specs=[smem, smem, pl.BlockSpec(memory_space=pltpu.VMEM)],
        out_specs=pl.BlockSpec(memory_space=pl.ANY),
        scratch_shapes=slab_scratch(per, SLOTS),
        compiler_params=pltpu.CompilerParams(has_side_effects=True, vmem_limit_bytes=60 << 20),
        name="gather_more",
    )(first, fill, panel)


def add_blocks(fill, base, first, t_hi, t_lo, slab, blocks, before, after):
    seen = jnp.int32(0)
    for b in range(blocks.shape[0]):
        before(b)
        for h in range(2):
            on = fill[h, base + b] != 0
            slot = seen - first

            @pl.when(jnp.logical_and(on, jnp.logical_and(slot >= 0, slot < SLOTS)))
            def _(b=b, h=h, slot=slot):
                m = split(jnp.concatenate([slab[slot, :, x].reshape(8 * ZS, B) for x in range(XS)], axis=0))
                t = (t_hi[B * h : B * h + B], t_lo[B * h : B * h + B])
                blocks[b] = blocks[b] - mm3(m, t, NN)

            seen = seen + jnp.where(on, 1, 0)
        after(b)


def update_kernel(fill_any, z, t_hi, t_lo, slab, panel, held, updated, own, most,
                  fill, blocks, in_sem, write_sem):
    col, row = lax.axis_index("col"), lax.axis_index("row")
    count = blocks.shape[0]
    base = count * row
    get_fill = local(fill_any, fill, in_sem)
    get_fill.start()
    get_fill.wait()

    def touched(b):
        return jnp.logical_or(fill[0, base + b] != 0, fill[1, base + b] != 0)

    def write(b):
        return local(blocks.at[b], updated.at[pl.ds(B * b, B)], write_sem.at[b])

    def keep(b):
        return local(held.at[pl.ds(B * b, B)], updated.at[pl.ds(B * b, B)], write_sem.at[b])

    for b in range(count):
        @pl.when(jnp.logical_not(touched(b)))
        def _(b=b):
            keep(b).start()

    top = jnp.int32(0)
    for r in range(ROWS):
        total = jnp.int32(0)
        for b in range(count):
            for h in range(2):
                total = total + jnp.where(fill[h, count * r + b] != 0, 1, 0)
        top = jnp.maximum(top, total)
    most[0] = top

    masked = []
    for t in range(panel.shape[0] // 8):
        block = base + (panel.shape[0] * col + 8 * t) // B
        masked.append(jnp.concatenate(
            [panel[8 * t : 8 * t + 8, B * h : B * h + B]
             * jnp.where(fill[h, block] != 0, 1.0, 0.0).astype(F32) for h in range(2)], axis=1))
    own[...] = mm(jnp.concatenate(masked, axis=0), z[...], NT)

    def before(b):
        @pl.when(touched(b))
        def _():
            blocks[b] = held[B * b : B * b + B]

    def after(b):
        @pl.when(touched(b))
        def _():
            write(b).start()

    add_blocks(fill, base, 0, t_hi, t_lo, slab, blocks, before, after)
    for b in range(count):
        write(b).wait()


def apply_update(fill, z, t_hi, t_lo, slab, panel, held):
    count = held.shape[0] // B
    width = held.shape[1]
    dma = pltpu.SemaphoreType.DMA
    vmem = pl.BlockSpec(memory_space=pltpu.VMEM)
    hbm = pl.BlockSpec(memory_space=pltpu.HBM)
    smem = pl.BlockSpec(memory_space=pltpu.SMEM)
    return pl.pallas_call(
        update_kernel,
        out_shape=(
            jax.ShapeDtypeStruct(held.shape, F32),
            jax.ShapeDtypeStruct(panel.shape, F32),
            jax.ShapeDtypeStruct((1,), jnp.int32),
        ),
        in_specs=[hbm, vmem, vmem, vmem, vmem, vmem, vmem],
        out_specs=(hbm, vmem, smem),
        scratch_shapes=[
            pltpu.SMEM(fill.shape, jnp.int32),
            pltpu.VMEM((count, B, width), F32),
            dma, dma((count,)),
        ],
        compiler_params=pltpu.CompilerParams(vmem_limit_bytes=30 << 20),
        name="apply_update",
    )(fill, z, t_hi, t_lo, slab, panel, held)


def update_more_kernel(first, fill, t_hi, t_lo, slab, before_any, after_any, blocks, read_sem, write_sem):
    count = blocks.shape[0]
    base = count * lax.axis_index("row")

    def read(b):
        return local(before_any.at[pl.ds(B * b, B)], blocks.at[b], read_sem.at[b])

    def write(b):
        return local(blocks.at[b], after_any.at[pl.ds(B * b, B)], write_sem.at[b])

    for b in range(count):
        read(b).start()
    add_blocks(fill, base, first[0], t_hi, t_lo, slab, blocks,
               lambda b: read(b).wait(), lambda b: write(b).start())
    for b in range(count):
        write(b).wait()


def update_more(first, fill, t_hi, t_lo, slab, updated):
    count = updated.shape[0] // B
    dma = pltpu.SemaphoreType.DMA
    vmem = pl.BlockSpec(memory_space=pltpu.VMEM)
    hbm = pl.BlockSpec(memory_space=pltpu.HBM)
    smem = pl.BlockSpec(memory_space=pltpu.SMEM)
    return pl.pallas_call(
        update_more_kernel,
        out_shape=jax.ShapeDtypeStruct(updated.shape, F32),
        in_specs=[smem, smem, vmem, vmem, vmem, hbm],
        out_specs=hbm,
        scratch_shapes=[
            pltpu.VMEM((count, B, updated.shape[1]), F32), dma((count,)), dma((count,))],
        input_output_aliases={5: 0},
        compiler_params=pltpu.CompilerParams(vmem_limit_bytes=60 << 20),
        name="update_more",
    )(first, fill, t_hi, t_lo, slab, updated)


def per_device(trailing, panel_rows, pivot_block, panel_fill):
    fill = panel_fill.T
    z, t_hi, t_lo, slab, held = gather_and_factor(fill, pivot_block, panel_rows, trailing)
    updated, own, most = apply_update(fill, z, t_hi, t_lo, slab, panel_rows, held)

    def body(state):
        first, updated = state
        more = gather_more(first, fill, panel_rows)
        return first + SLOTS, update_more(first, fill, t_hi, t_lo, more, updated)

    start = jnp.full((1,), SLOTS, jnp.int32)
    _, updated = lax.while_loop(lambda state: state[0][0] < most[0], body, (start, updated))
    return updated, own


def solution(mesh):
    in_specs = (P("row", "col"), P(("row", "col"), None), P("col", None), P())
    out_specs = (P("row", "col"), P(("row", "col"), None))
    return jax.shard_map(
        per_device, mesh=mesh, in_specs=in_specs, out_specs=out_specs, check_vma=False
    )
```

```python
import functools

import jax
import jax.numpy as jnp
from jax import lax
from jax.experimental import pallas as pl
from jax.experimental.pallas import tpu as pltpu
from jax.sharding import PartitionSpec as P

F32 = jnp.float32
BF16 = jnp.bfloat16
HIGHEST = lax.Precision.HIGHEST
NT = (((1,), (1,)), ((), ()))
NN = (((1,), (0,)), ((), ()))
TN = (((0,), (0,)), ((), ()))

ZS, XS = 8, 4
COLS, ROWS = ZS * XS, 8
B = 256
TILE = 128


def mm(a, b, dims):
    return lax.dot_general(a, b, dims, precision=HIGHEST, preferred_element_type=F32)


def split(v):
    hi = v.astype(BF16)
    return hi, (v - hi.astype(F32)).astype(BF16)


def mm3(a, b, dims):
    dot = functools.partial(lax.dot_general, dimension_numbers=dims, preferred_element_type=F32)
    return dot(a[0], b[0]) + (dot(a[0], b[1]) + dot(a[1], b[0]))


def spread_row(v, r):
    return jnp.broadcast_to(v[r : r + 1, :], v.shape)


def invert_tile(groups, hook):
    n = groups[0].shape[1]
    count = n // 8
    lane = lax.broadcasted_iota(jnp.int32, (8, n), 1)
    sub = lax.broadcasted_iota(jnp.int32, (8, n), 0)
    left = list(groups)
    right = [jnp.where(lane == sub + 8 * g, 1.0, 0.0).astype(F32) for g in range(count)]
    done = []

    def columns(h, g):
        return [
            jnp.broadcast_to(left[h][:, 8 * g + r : 8 * g + r + 1], (8, n)) for r in range(8)
        ]

    def total(terms):
        while len(terms) > 1:
            terms = [a + b for a, b in zip(terms[::2], terms[1::2])]
        return terms[0]

    for g in range(count):
        hook(g)
        pivot = columns(g, g)
        below = {h: columns(h, g) for h in range(g + 1, count)}
        wide, inv = left[g], right[g]
        final = inv
        for r in range(0, 8, 2):
            a, b, d = (
                spread_row(pivot[r], r),
                spread_row(pivot[r + 1], r),
                spread_row(pivot[r + 1], r + 1),
            )
            det = a * d - b * b
            scale = 1.0 / det
            an, bn, dn = a * scale, b * scale, d * scale
            m0, m1 = pivot[r], pivot[r + 1]
            e0, e1 = spread_row(inv, r), spread_row(inv, r + 1)
            over_a = 1.0 / a
            f0 = e0 * lax.rsqrt(a)
            f1 = (e1 - (b * over_a) * e0) * lax.rsqrt(det * over_a)
            final = jnp.where(sub == r, f0, jnp.where(sub == r + 1, f1, final))

            def step(w):
                w0, w1 = spread_row(w, r), spread_row(w, r + 1)
                y0 = dn * w0 - bn * w1
                y1 = an * w1 - bn * w0
                rest = w - (m0 * y0 + m1 * y1)
                return jnp.where(sub == r, y0, jnp.where(sub == r + 1, y1, rest))

            for q in range(r + 2, 8):
                pivot[q] = step(pivot[q])
            wide, inv = step(wide), step(inv)
        done.append(final)
        wide_rows = [spread_row(wide, r) for r in range(8)]
        inv_rows = [spread_row(inv, r) for r in range(8)]
        for h in range(g + 1, count):
            left[h] = left[h] - total([below[h][r] * wide_rows[r] for r in range(8)])
            right[h] = right[h] - total([below[h][r] * inv_rows[r] for r in range(8)])
    return done

SLOTS = 8


def remote(src, dst, send, recv, col, row):
    return pltpu.make_async_remote_copy(
        src_ref=src, dst_ref=dst, send_sem=send, recv_sem=recv,
        device_id={"col": col, "row": row}, device_id_type=pl.DeviceIdType.MESH)


local = pltpu.make_async_copy


def place():
    col, row = lax.axis_index("col"), lax.axis_index("row")
    return col, row, col // XS, col % XS, row // 2, row % 2


def slots_of(fill, base, first, slots, halves):
    where = [jnp.int32(0)] * slots
    seen = jnp.int32(0)
    for n in range(halves):
        on = fill[n % 2, base + n // 2] != 0
        for k in range(slots):
            hit = jnp.logical_and(on, seen == first + k)
            where[k] = jnp.where(hit, n, where[k])
        seen = seen + jnp.where(on, 1, 0)
    return where


class SlabGather:
    def __init__(self, staged, queued, packed, slab, q_send, q_recv, x_send, x_recv, x_own, r_send, r_recv):
        self.refs = staged, queued, packed, slab
        self.q_send, self.q_recv, self.x_own = q_send, q_recv, x_own
        self.x_send, self.x_recv, self.r_send, self.r_recv = x_send, x_recv, r_send, r_recv
        self.slots = packed.shape[0]
        self.per = staged.shape[0]

    def stage(self, panel):
        staged = self.refs[0]
        for t in range(self.per):
            for h in range(2):
                staged[t, h] = panel[8 * t : 8 * t + 8, B * h : B * h + B]

    def target(self, t):
        index = self.per * place()[0] + t
        return index // COLS, (index % ZS) * XS + (index % COLS) // ZS

    def spread(self):
        staged, queued, _, _ = self.refs
        col, row, *_ = place()

        def send(t, _):
            block, target = self.target(t)
            there = queued.at[pl.ds(2 * block, 2)]

            @pl.when(target != col)
            def _():
                remote(staged.at[t], there, self.q_send, self.q_recv, target, row).start()

            @pl.when(target == col)
            def _():
                local(staged.at[t], there, self.q_recv).start()
            return 0

        lax.fori_loop(0, self.per, send, 0)

    def along_x(self, dx):
        _, _, packed, slab = self.refs
        col, row, zi, xi, *_ = place()
        half = self.slots // 2
        return remote(packed.at[pl.ds(0, half)], slab.at[pl.ds(0, half), zi, xi],
                      self.x_send.at[dx - 1], self.x_recv.at[dx - 1], zi * XS + (xi + dx) % XS, row)

    def across_x(self, z, start, count, dx):
        slab = self.refs[3]
        col, row, zi, xi, *_ = place()
        part = slab.at[pl.ds(start, count), z, xi]
        return remote(part, part, self.x_send.at[dx + 2], self.x_recv.at[dx + 2],
                      zi * XS + (xi + dx) % XS, row)

    def pass_across(self, z):
        half = self.slots // 2
        for dx in range(1, XS):
            self.across_x(z, half, half, dx).start()

    def own(self):
        _, _, packed, slab = self.refs
        _, _, zi, xi, *_ = place()
        return local(packed, slab.at[:, zi, xi], self.x_own)

    def pack(self, where):
        _, queued, packed, _ = self.refs
        zi = place()[2]
        local(queued, queued, self.q_recv).wait()
        for k in range(self.slots):
            packed[k] = queued[where[k]]
        self.own().start()
        for dx in range(1, XS):
            self.along_x(dx).start()
        self.own().wait()
        for side in range(2):
            self.ring(1, 0, side).start()
        self.pass_across(zi)

    def source(self, step, side):
        sign = 1 if side == 0 else -1
        return (place()[2] - sign * step + ZS) % ZS

    def ring(self, kind, step, side):
        slab = self.refs[3]
        col, row, zi, xi, *_ = place()
        sign = 1 if side == 0 else -1
        half = self.slots // 2
        rows = pl.ds(kind * half, half) if step < 3 else pl.ds(kind * half + side * (half // 2), half // 2)
        part = slab.at[rows, self.source(step, side)] if kind == 0 else slab.at[rows, self.source(step, side), xi]
        target = ((zi + sign + ZS) % ZS) * XS + xi
        return remote(part, part, self.r_send.at[kind, side, step], self.r_recv.at[kind, side, step], target, row)

    def first(self):
        for dx in range(1, XS):
            self.along_x(dx).wait_recv()
        for side in range(2):
            self.ring(0, 0, side).start()
        self.next_across(1)

    def next_across(self, step):
        for side in range(2):
            self.ring(1, step - 1, side).wait_recv()
            if step < 4:
                self.ring(1, step, side).start()
        if step < 4:
            for side in range(2):
                self.pass_across(self.source(step, side))
        else:
            self.pass_across(self.source(4, 0))

    def next(self, step):
        for side in range(2):
            self.ring(0, step - 1, side).wait_recv()
            self.ring(0, step, side).start()
        self.next_across(step + 1)

    def last(self):
        staged, _, _, slab = self.refs
        half = self.slots // 2
        col = place()[0]
        for side in range(2):
            self.ring(0, 3, side).wait_recv()
        line = slab.at[pl.ds(half, half), :, 0]
        for dx in range(1, XS):
            local(line, line, self.x_recv.at[dx + 2]).wait()
            local(line, line, self.x_send.at[dx + 2]).wait()
            self.along_x(dx).wait_send()
        for kind in range(2):
            for side in range(2):
                for step in range(4):
                    self.ring(kind, step, side).wait_send()

        def sent(t, _):
            @pl.when(self.target(t)[1] != col)
            def _():
                local(staged.at[0], staged.at[0], self.q_send).wait()
            return 0

        lax.fori_loop(0, self.per, sent, 0)


def slab_scratch(per, slots):
    dma = pltpu.SemaphoreType.DMA
    return [
        pltpu.VMEM((per, 2, 8, B), F32), pltpu.VMEM((2 * per, 8, B), F32), pltpu.VMEM((slots, 8, B), F32),
        dma, dma, dma((6,)), dma((6,)), dma, dma((2, 2, 4)), dma((2, 2, 4)),
    ]


def gather_kernel(fill_any, pivot_any, panel_any, z_out, t_hi, t_lo, slab, fill, pivot, panel, work, full, mc,
                  in_sem, zs_send, zs_recv, zx_send, zx_recv, ex_send, ex_recv, c_send, c_recv,
                  y_send, y_recv, k_send, k_recv, staged, queued, packed, *slab_sems):
    col, row, zi, xi, y, core = place()
    halves = queued.shape[0]
    per = staged.shape[0]
    blocks = halves // 2
    gather = SlabGather(staged, queued, packed, slab, *slab_sems)
    loads = [
        local(fill_any, fill, in_sem.at[0]),
        local(pivot_any, pivot, in_sem.at[1]),
        local(panel_any, panel, in_sem.at[2]),
    ]
    for load in loads:
        load.start()

    def column_target(t):
        index = per * col + t
        target_col, target_row = 6 * row + index // 64, index % 8
        own = jnp.logical_and(target_col == col, target_row == row)
        return (index % 64) // 8, target_col, target_row, own

    def column_sends(t):
        _, target_col, _, own = column_target(t)
        return jnp.logical_and(target_col < COLS, jnp.logical_not(own))

    barrier = pltpu.get_barrier_semaphore()

    def greet(c, r):
        pl.semaphore_signal(barrier, inc=1, device_id={"col": c, "row": r}, device_id_type=pl.DeviceIdType.MESH)

    def greet_slab(i, _):
        greet((col + i) % COLS, row)
        return 0

    lax.fori_loop(1, COLS, greet_slab, 0)
    greet(col, 2 * y + 1 - core)
    for dy in range(1, 4):
        greet(col, 2 * ((y + dy) % 4) + core)

    def greet_column(s, _):
        source = (64 * (col % 6) + 8 * s + row) // per
        source_row = col // 6

        @pl.when(jnp.logical_not(jnp.logical_and(source == col, source_row == row)))
        def _():
            greet(source, source_row)
        return 0

    lax.fori_loop(0, 8, greet_column, 0)
    expected = jnp.int32(COLS - 1 + 4)
    for t in range(per):
        expected = expected + jnp.where(column_sends(t), 1, 0)
    z_out[...] = jnp.zeros_like(z_out)
    for load in loads:
        load.wait()
    gather.stage(panel)
    pl.semaphore_wait(barrier, expected)

    def pivot_z(dz):
        target = ((zi + dz) % ZS) * XS + xi
        return remote(pivot.at[core], full.at[zi, xi, core], zs_send, zs_recv.at[zi], target, row)

    def pivot_from(z):
        part = full.at[z, xi, core]
        return local(part, part, zs_recv.at[z])

    def pivot_x(part, dx):
        rows = full.at[pl.ds(0, 2), xi, core] if part == 0 else full.at[pl.ds(2, ZS - 2), xi, core]
        return remote(rows, rows, zx_send.at[part, dx - 1], zx_recv.at[part, dx - 1],
                      zi * XS + (xi + dx) % XS, row)

    def exchange(part):
        rows = full.at[pl.ds(0, 2), :, core] if part == 0 else full.at[pl.ds(2, ZS - 2), :, core]
        return remote(rows, rows, ex_send.at[part], ex_recv.at[part], col, 2 * y + 1 - core)

    local(pivot.at[core], full.at[zi, xi, core], zs_recv.at[zi]).start()
    for dz in (4, 3, 5, 2, 6, 1, 7):
        pivot_z(dz).start()
    gather.spread()

    def send_column(t, _):
        slot, target_col, target_row, own = column_target(t)
        there = mc.at[slot, target_row]

        @pl.when(column_sends(t))
        def _():
            remote(staged.at[t], there, c_send, c_recv, target_col, target_row).start()

        @pl.when(own)
        def _():
            local(staged.at[t], there, c_recv).start()
        return 0

    lax.fori_loop(0, per, send_column, 0)
    where = slots_of(fill, blocks * row, 0, SLOTS, halves)
    for z in range(2):
        pivot_from(z).wait()
    for dx in range(1, XS):
        pivot_x(0, dx).start()
    for z in range(2, ZS):
        pivot_from(z).wait()
    for dx in range(1, XS):
        pivot_x(1, dx).start()
    gather.pack(where)
    for dx in range(1, XS):
        pivot_x(0, dx).wait_recv()
    exchange(0).start()
    def pivot_rest():
        for dx in range(1, XS):
            pivot_x(1, dx).wait_recv()
        exchange(1).start()

    def column_y(dy):
        part = mc.at[:, row]
        return remote(part, part, y_send.at[dy - 1], y_recv.at[dy - 1], col, 2 * ((y + dy) % 4) + core)

    def column_first():
        part = mc.at[:, row]
        local(part, part, c_recv).wait()
        for dy in range(1, 4):
            column_y(dy).start()

    def column_core(i):
        part = mc.at[:, 2 * i + core]
        return remote(part, part, k_send.at[i], k_recv.at[i], col, 2 * y + 1 - core)

    def column_next():
        for dy in range(1, 4):
            column_y(dy).wait_recv()
        for i in range(4):
            column_core(i).start()

    plan = {
        (0, 3): pivot_rest,
        (0, 4): gather.first,
        (0, 11): column_first,
        (1, 2): functools.partial(gather.next, 1),
        (1, 15): functools.partial(gather.next, 2),
        (2, 6): column_next,
        (2, 14): functools.partial(gather.next, 3),
    }

    n = z_out.shape[0]
    exchange(0).wait_recv()
    for k in range(n // TILE):
        lo, hi = k * TILE, (k + 1) * TILE
        if k == 0:
            groups = [full[g // 8, (g // 2) % 4, g % 2, :, lo:hi] for g in range(TILE // 8)]
        else:
            groups = [work[lo + 8 * g : lo + 8 * g + 8, lo:hi] for g in range(TILE // 8)]

        def hook(g, k=k):
            if (k, g) in plan:
                plan[k, g]()

        rows = invert_tile(groups, hook)
        for g in range(TILE // 8):
            z_out[lo + 8 * g : lo + 8 * g + 8, lo:hi] = rows[g]
        zk = z_out[lo:hi, lo:hi]
        if k > 0:
            z_out[lo:hi, :lo] = mm(zk, z_out[lo:hi, :lo], NN)
        if hi < n:
            if k == 0:
                exchange(1).wait_recv()
                below = full[2:].reshape(n - hi, n)
            else:
                below = work[hi:, :]
            p = mm(below[:, lo:hi], zk, NT)
            work[hi:, hi:] = below[:, hi:] - mm(p, p, NT)
            z_out[hi:, :hi] = z_out[hi:, :hi] - mm(p, z_out[lo:hi, :hi], NN)

    for i in range(4):
        column_core(i).wait_recv()

    def flag(block, h):
        return jnp.where(fill[h, block] != 0, 1.0, 0.0).astype(F32)

    rows = []
    for i in range(2):
        part = mc[4 * i : 4 * i + 4]
        rows.append(jnp.concatenate(
            [part[:, :, h].reshape(B, B) * flag(2 * col + i, h) for h in range(2)], axis=1))
    zs = split(z_out[...])
    xc = mm3(zs, split(jnp.concatenate(rows, axis=0)), NT)
    t_hi[...], t_lo[...] = split(mm3(zs, split(xc), TN))

    gather.last()
    for i in range(4):
        column_core(i).wait_send()
    for dy in range(1, 4):
        column_y(dy).wait_send()
    for part in range(2):
        exchange(part).wait_send()
        for dx in range(1, XS):
            pivot_x(part, dx).wait_send()
    local(full.at[pl.ds(0, ZS - 1), 0, core], full.at[pl.ds(0, ZS - 1), 0, core], zs_send).wait()

    def sent_column(t, _):
        @pl.when(column_sends(t))
        def _():
            local(staged.at[0], staged.at[0], c_send).wait()
        return 0

    lax.fori_loop(0, per, sent_column, 0)


def gather_and_factor(fill, pivot, panel):
    n = panel.shape[1]
    per = panel.shape[0] // 8
    dma = pltpu.SemaphoreType.DMA
    vmem = pl.BlockSpec(memory_space=pltpu.VMEM)
    anywhere = pl.BlockSpec(memory_space=pl.ANY)
    return pl.pallas_call(
        gather_kernel,
        out_shape=(
            jax.ShapeDtypeStruct((n, n), F32),
            jax.ShapeDtypeStruct((n, n), BF16),
            jax.ShapeDtypeStruct((n, n), BF16),
            jax.ShapeDtypeStruct((SLOTS, ZS, XS, 8, B), F32),
        ),
        in_specs=[pl.BlockSpec(memory_space=pltpu.HBM)] * 3,
        out_specs=(vmem, vmem, vmem, anywhere),
        scratch_shapes=[
            pltpu.SMEM(fill.shape, jnp.int32),
            pltpu.VMEM((2, 8, n), F32),
            pltpu.VMEM(panel.shape, F32),
            pltpu.VMEM((n, n), F32),
            pltpu.VMEM((ZS, XS, 2, 8, n), F32),
            pltpu.VMEM((8, ROWS, 2, 8, B), F32),
            dma((3,)), dma, dma((ZS,)), dma((2, 3)), dma((2, 3)), dma((2,)), dma((2,)), dma, dma,
            dma((3,)), dma((3,)), dma((4,)), dma((4,)),
        ] + slab_scratch(per, SLOTS),
        compiler_params=pltpu.CompilerParams(
            has_side_effects=True, collective_id=0, vmem_limit_bytes=30 << 20),
        cost_estimate=pl.CostEstimate(flops=40_000_000_000, bytes_accessed=60_000_000, transcendentals=0),
        name="gather_and_factor",
    )(fill, pivot.reshape(2, 8, n), panel)


def gather_more_kernel(first, fill, panel, slab, staged, queued, packed, *sems):
    row = lax.axis_index("row")
    halves = queued.shape[0]
    gather = SlabGather(staged, queued, packed, slab, *sems)
    gather.stage(panel)
    gather.spread()
    gather.pack(slots_of(fill, halves // 2 * row, first[0], SLOTS, halves))
    gather.first()
    for step in range(1, 4):
        gather.next(step)
    gather.last()


def gather_more(first, fill, panel):
    per = panel.shape[0] // 8
    smem = pl.BlockSpec(memory_space=pltpu.SMEM)
    return pl.pallas_call(
        gather_more_kernel,
        out_shape=jax.ShapeDtypeStruct((SLOTS, ZS, XS, 8, B), F32),
        in_specs=[smem, smem, pl.BlockSpec(memory_space=pltpu.VMEM)],
        out_specs=pl.BlockSpec(memory_space=pl.ANY),
        scratch_shapes=slab_scratch(per, SLOTS),
        compiler_params=pltpu.CompilerParams(has_side_effects=True, vmem_limit_bytes=60 << 20),
        name="gather_more",
    )(first, fill, panel)


def add_blocks(fill, base, first, t_hi, t_lo, slab, blocks, before, after):
    seen = jnp.int32(0)
    for b in range(blocks.shape[0]):
        before(b)
        for h in range(2):
            on = fill[h, base + b] != 0
            slot = seen - first

            @pl.when(jnp.logical_and(on, jnp.logical_and(slot >= 0, slot < SLOTS)))
            def _(b=b, h=h, slot=slot):
                m = split(jnp.concatenate([slab[slot, :, x].reshape(8 * ZS, B) for x in range(XS)], axis=0))
                t = (t_hi[B * h : B * h + B], t_lo[B * h : B * h + B])
                blocks[b] = blocks[b] - mm3(m, t, NN)

            seen = seen + jnp.where(on, 1, 0)
        after(b)


def update_kernel(fill_any, z, t_hi, t_lo, slab, panel, held, updated, own, most,
                  fill, blocks, in_sem, write_sem):
    col, row = lax.axis_index("col"), lax.axis_index("row")
    count = blocks.shape[0]
    base = count * row
    get_fill = local(fill_any, fill, in_sem)
    get_fill.start()
    get_fill.wait()

    def touched(b):
        return jnp.logical_or(fill[0, base + b] != 0, fill[1, base + b] != 0)

    def write(b):
        return local(blocks.at[b], updated.at[pl.ds(B * b, B)], write_sem.at[b])

    def keep(b):
        return local(held.at[pl.ds(B * b, B)], updated.at[pl.ds(B * b, B)], write_sem.at[b])

    for b in range(count):
        @pl.when(jnp.logical_not(touched(b)))
        def _(b=b):
            keep(b).start()

    top = jnp.int32(0)
    for r in range(ROWS):
        total = jnp.int32(0)
        for b in range(count):
            for h in range(2):
                total = total + jnp.where(fill[h, count * r + b] != 0, 1, 0)
        top = jnp.maximum(top, total)
    most[0] = top

    masked = []
    for t in range(panel.shape[0] // 8):
        block = base + (panel.shape[0] * col + 8 * t) // B
        masked.append(jnp.concatenate(
            [panel[8 * t : 8 * t + 8, B * h : B * h + B]
             * jnp.where(fill[h, block] != 0, 1.0, 0.0).astype(F32) for h in range(2)], axis=1))
    own[...] = mm(jnp.concatenate(masked, axis=0), z[...], NT)

    def before(b):
        @pl.when(touched(b))
        def _():
            blocks[b] = held[B * b : B * b + B]

    def after(b):
        @pl.when(touched(b))
        def _():
            write(b).start()

    add_blocks(fill, base, 0, t_hi, t_lo, slab, blocks, before, after)
    for b in range(count):
        write(b).wait()


def apply_update(fill, z, t_hi, t_lo, slab, panel, held):
    count = held.shape[0] // B
    width = held.shape[1]
    dma = pltpu.SemaphoreType.DMA
    vmem = pl.BlockSpec(memory_space=pltpu.VMEM)
    hbm = pl.BlockSpec(memory_space=pltpu.HBM)
    smem = pl.BlockSpec(memory_space=pltpu.SMEM)
    return pl.pallas_call(
        update_kernel,
        out_shape=(
            jax.ShapeDtypeStruct(held.shape, F32),
            jax.ShapeDtypeStruct(panel.shape, F32),
            jax.ShapeDtypeStruct((1,), jnp.int32),
        ),
        in_specs=[hbm, vmem, vmem, vmem, vmem, vmem, vmem],
        out_specs=(hbm, vmem, smem),
        scratch_shapes=[
            pltpu.SMEM(fill.shape, jnp.int32),
            pltpu.VMEM((count, B, width), F32),
            dma, dma((count,)),
        ],
        compiler_params=pltpu.CompilerParams(vmem_limit_bytes=30 << 20),
        name="apply_update",
    )(fill, z, t_hi, t_lo, slab, panel, held)


def update_more_kernel(first, fill, t_hi, t_lo, slab, before_any, after_any, blocks, read_sem, write_sem):
    count = blocks.shape[0]
    base = count * lax.axis_index("row")

    def read(b):
        return local(before_any.at[pl.ds(B * b, B)], blocks.at[b], read_sem.at[b])

    def write(b):
        return local(blocks.at[b], after_any.at[pl.ds(B * b, B)], write_sem.at[b])

    for b in range(count):
        read(b).start()
    add_blocks(fill, base, first[0], t_hi, t_lo, slab, blocks,
               lambda b: read(b).wait(), lambda b: write(b).start())
    for b in range(count):
        write(b).wait()


def update_more(first, fill, t_hi, t_lo, slab, updated):
    count = updated.shape[0] // B
    dma = pltpu.SemaphoreType.DMA
    vmem = pl.BlockSpec(memory_space=pltpu.VMEM)
    hbm = pl.BlockSpec(memory_space=pltpu.HBM)
    smem = pl.BlockSpec(memory_space=pltpu.SMEM)
    return pl.pallas_call(
        update_more_kernel,
        out_shape=jax.ShapeDtypeStruct(updated.shape, F32),
        in_specs=[smem, smem, vmem, vmem, vmem, hbm],
        out_specs=hbm,
        scratch_shapes=[
            pltpu.VMEM((count, B, updated.shape[1]), F32), dma((count,)), dma((count,))],
        input_output_aliases={5: 0},
        compiler_params=pltpu.CompilerParams(vmem_limit_bytes=60 << 20),
        name="update_more",
    )(first, fill, t_hi, t_lo, slab, updated)


def per_device(trailing, panel_rows, pivot_block, panel_fill):
    fill = panel_fill.T
    z, t_hi, t_lo, slab = gather_and_factor(fill, pivot_block, panel_rows)
    updated, own, most = apply_update(fill, z, t_hi, t_lo, slab, panel_rows, trailing)

    def body(state):
        first, updated = state
        more = gather_more(first, fill, panel_rows)
        return first + SLOTS, update_more(first, fill, t_hi, t_lo, more, updated)

    start = jnp.full((1,), SLOTS, jnp.int32)
    _, updated = lax.while_loop(lambda state: state[0][0] < most[0], body, (start, updated))
    return updated, own


def solution(mesh):
    in_specs = (P("row", "col"), P(("row", "col"), None), P("col", None), P())
    out_specs = (P("row", "col"), P(("row", "col"), None))
    return jax.shard_map(
        per_device, mesh=mesh, in_specs=in_specs, out_specs=out_specs, check_vma=False
    )
```

```python
import functools

import jax
import jax.numpy as jnp
from jax import lax
from jax.experimental import pallas as pl
from jax.experimental.pallas import tpu as pltpu
from jax.sharding import PartitionSpec as P

F32 = jnp.float32
BF16 = jnp.bfloat16
HIGHEST = lax.Precision.HIGHEST
NT = (((1,), (1,)), ((), ()))
NN = (((1,), (0,)), ((), ()))
TN = (((0,), (0,)), ((), ()))

ZS, XS = 8, 4
COLS, ROWS = ZS * XS, 8
B = 256
TILE = 128


def mm(a, b, dims):
    return lax.dot_general(a, b, dims, precision=HIGHEST, preferred_element_type=F32)


def split(v):
    hi = v.astype(BF16)
    return hi, (v - hi.astype(F32)).astype(BF16)


def mm3(a, b, dims):
    dot = functools.partial(lax.dot_general, dimension_numbers=dims, preferred_element_type=F32)
    return dot(a[0], b[0]) + (dot(a[0], b[1]) + dot(a[1], b[0]))


def spread_row(v, r):
    return jnp.broadcast_to(v[r : r + 1, :], v.shape)


def invert_tile(groups, hook):
    n = groups[0].shape[1]
    count = n // 8
    lane = lax.broadcasted_iota(jnp.int32, (8, n), 1)
    sub = lax.broadcasted_iota(jnp.int32, (8, n), 0)
    left = list(groups)
    right = [jnp.where(lane == sub + 8 * g, 1.0, 0.0).astype(F32) for g in range(count)]
    done = []

    def columns(h, g):
        return [
            jnp.broadcast_to(left[h][:, 8 * g + r : 8 * g + r + 1], (8, n)) for r in range(8)
        ]

    def total(terms):
        while len(terms) > 1:
            terms = [a + b for a, b in zip(terms[::2], terms[1::2])]
        return terms[0]

    for g in range(count):
        hook(g)
        pivot = columns(g, g)
        below = {h: columns(h, g) for h in range(g + 1, count)}
        wide, inv = left[g], right[g]
        final = inv
        for r in range(0, 8, 2):
            a, b, d = (
                spread_row(pivot[r], r),
                spread_row(pivot[r + 1], r),
                spread_row(pivot[r + 1], r + 1),
            )
            det = a * d - b * b
            scale = 1.0 / det
            an, bn, dn = a * scale, b * scale, d * scale
            m0, m1 = pivot[r], pivot[r + 1]
            e0, e1 = spread_row(inv, r), spread_row(inv, r + 1)
            over_a = 1.0 / a
            f0 = e0 * lax.rsqrt(a)
            f1 = (e1 - (b * over_a) * e0) * lax.rsqrt(det * over_a)
            final = jnp.where(sub == r, f0, jnp.where(sub == r + 1, f1, final))

            def step(w):
                w0, w1 = spread_row(w, r), spread_row(w, r + 1)
                y0 = dn * w0 - bn * w1
                y1 = an * w1 - bn * w0
                rest = w - (m0 * y0 + m1 * y1)
                return jnp.where(sub == r, y0, jnp.where(sub == r + 1, y1, rest))

            for q in range(r + 2, 8):
                pivot[q] = step(pivot[q])
            wide, inv = step(wide), step(inv)
        done.append(final)
        wide_rows = [spread_row(wide, r) for r in range(8)]
        inv_rows = [spread_row(inv, r) for r in range(8)]
        for h in range(g + 1, count):
            left[h] = left[h] - total([below[h][r] * wide_rows[r] for r in range(8)])
            right[h] = right[h] - total([below[h][r] * inv_rows[r] for r in range(8)])
    return done

SLOTS = 8


def remote(src, dst, send, recv, col, row):
    return pltpu.make_async_remote_copy(
        src_ref=src, dst_ref=dst, send_sem=send, recv_sem=recv,
        device_id={"col": col, "row": row}, device_id_type=pl.DeviceIdType.MESH)


local = pltpu.make_async_copy


def place():
    col, row = lax.axis_index("col"), lax.axis_index("row")
    return col, row, col // XS, col % XS, row // 2, row % 2


def slots_of(fill, base, first, slots, halves):
    where = [jnp.int32(0)] * slots
    seen = jnp.int32(0)
    for n in range(halves):
        on = fill[n % 2, base + n // 2] != 0
        for k in range(slots):
            hit = jnp.logical_and(on, seen == first + k)
            where[k] = jnp.where(hit, n, where[k])
        seen = seen + jnp.where(on, 1, 0)
    return where


class SlabGather:
    def __init__(self, staged, queued, packed, slab, q_send, q_recv, x_send, x_recv, x_own, r_send, r_recv):
        self.refs = staged, queued, packed, slab
        self.q_send, self.q_recv, self.x_own = q_send, q_recv, x_own
        self.x_send, self.x_recv, self.r_send, self.r_recv = x_send, x_recv, r_send, r_recv
        self.slots = packed.shape[0]
        self.per = staged.shape[0]

    def stage(self, panel):
        staged = self.refs[0]
        for t in range(self.per):
            for h in range(2):
                staged[t, h] = panel[8 * t : 8 * t + 8, B * h : B * h + B]

    def target(self, t):
        index = self.per * place()[0] + t
        return index // COLS, (index % ZS) * XS + (index % COLS) // ZS

    def spread(self):
        staged, queued, _, _ = self.refs
        col, row, *_ = place()

        def send(t, _):
            block, target = self.target(t)
            there = queued.at[pl.ds(2 * block, 2)]

            @pl.when(target != col)
            def _():
                remote(staged.at[t], there, self.q_send, self.q_recv, target, row).start()

            @pl.when(target == col)
            def _():
                local(staged.at[t], there, self.q_recv).start()
            return 0

        lax.fori_loop(0, self.per, send, 0)

    def along_x(self, dx):
        _, _, packed, slab = self.refs
        col, row, zi, xi, *_ = place()
        half = self.slots // 2
        return remote(packed.at[pl.ds(0, half)], slab.at[pl.ds(0, half), zi, xi],
                      self.x_send.at[dx - 1], self.x_recv.at[dx - 1], zi * XS + (xi + dx) % XS, row)

    def across_x(self, z, start, count, dx):
        slab = self.refs[3]
        col, row, zi, xi, *_ = place()
        part = slab.at[pl.ds(start, count), z, xi]
        return remote(part, part, self.x_send.at[dx + 2], self.x_recv.at[dx + 2],
                      zi * XS + (xi + dx) % XS, row)

    def pass_across(self, z):
        half = self.slots // 2
        for dx in range(1, XS):
            self.across_x(z, half, half, dx).start()

    def own(self):
        _, _, packed, slab = self.refs
        _, _, zi, xi, *_ = place()
        return local(packed, slab.at[:, zi, xi], self.x_own)

    def pack(self, where):
        _, queued, packed, _ = self.refs
        zi = place()[2]
        local(queued, queued, self.q_recv).wait()
        for k in range(self.slots):
            packed[k] = queued[where[k]]
        self.own().start()
        for dx in range(1, XS):
            self.along_x(dx).start()
        self.own().wait()
        for side in range(2):
            self.ring(1, 0, side).start()
        self.pass_across(zi)

    def source(self, step, side):
        sign = 1 if side == 0 else -1
        return (place()[2] - sign * step + ZS) % ZS

    def ring(self, kind, step, side):
        slab = self.refs[3]
        col, row, zi, xi, *_ = place()
        sign = 1 if side == 0 else -1
        half = self.slots // 2
        rows = pl.ds(kind * half, half) if step < 3 else pl.ds(kind * half + side * (half // 2), half // 2)
        part = slab.at[rows, self.source(step, side)] if kind == 0 else slab.at[rows, self.source(step, side), xi]
        target = ((zi + sign + ZS) % ZS) * XS + xi
        return remote(part, part, self.r_send.at[kind, side, step], self.r_recv.at[kind, side, step], target, row)

    def first(self):
        for dx in range(1, XS):
            self.along_x(dx).wait_recv()
        for side in range(2):
            self.ring(0, 0, side).start()
        self.next_across(1)

    def next_across(self, step):
        for side in range(2):
            self.ring(1, step - 1, side).wait_recv()
            if step < 4:
                self.ring(1, step, side).start()
        if step < 4:
            for side in range(2):
                self.pass_across(self.source(step, side))
        else:
            self.pass_across(self.source(4, 0))

    def next(self, step):
        for side in range(2):
            self.ring(0, step - 1, side).wait_recv()
            self.ring(0, step, side).start()
        self.next_across(step + 1)

    def last(self):
        staged, _, _, slab = self.refs
        half = self.slots // 2
        col = place()[0]
        for side in range(2):
            self.ring(0, 3, side).wait_recv()
        line = slab.at[pl.ds(half, half), :, 0]
        for dx in range(1, XS):
            local(line, line, self.x_recv.at[dx + 2]).wait()
            local(line, line, self.x_send.at[dx + 2]).wait()
            self.along_x(dx).wait_send()
        for kind in range(2):
            for side in range(2):
                for step in range(4):
                    self.ring(kind, step, side).wait_send()

        def sent(t, _):
            @pl.when(self.target(t)[1] != col)
            def _():
                local(staged.at[0], staged.at[0], self.q_send).wait()
            return 0

        lax.fori_loop(0, self.per, sent, 0)


def slab_scratch(per, slots):
    dma = pltpu.SemaphoreType.DMA
    return [
        pltpu.VMEM((per, 2, 8, B), F32), pltpu.VMEM((2 * per, 8, B), F32), pltpu.VMEM((slots, 8, B), F32),
        dma, dma, dma((6,)), dma((6,)), dma, dma((2, 2, 4)), dma((2, 2, 4)),
    ]


def gather_kernel(fill_any, pivot_any, panel_any, z_out, t_hi, t_lo, slab, fill, pivot, panel, work, full, mc,
                  in_sem, zs_send, zs_recv, zx_send, zx_recv, ex_send, ex_recv, c_send, c_recv,
                  y_send, y_recv, k_send, k_recv, staged, queued, packed, *slab_sems):
    col, row, zi, xi, y, core = place()
    halves = queued.shape[0]
    per = staged.shape[0]
    blocks = halves // 2
    gather = SlabGather(staged, queued, packed, slab, *slab_sems)
    loads = [
        local(fill_any, fill, in_sem.at[0]),
        local(pivot_any, pivot, in_sem.at[1]),
        local(panel_any, panel, in_sem.at[2]),
    ]
    for load in loads:
        load.start()

    def column_target(t):
        index = per * col + t
        target_col, target_row = 6 * row + index // 64, index % 8
        own = jnp.logical_and(target_col == col, target_row == row)
        return (index % 64) // 8, target_col, target_row, own

    def column_sends(t):
        _, target_col, _, own = column_target(t)
        return jnp.logical_and(target_col < COLS, jnp.logical_not(own))

    barrier = pltpu.get_barrier_semaphore()

    def greet(c, r):
        pl.semaphore_signal(barrier, inc=1, device_id={"col": c, "row": r}, device_id_type=pl.DeviceIdType.MESH)

    def greet_slab(i, _):
        greet((col + i) % COLS, row)
        return 0

    lax.fori_loop(1, COLS, greet_slab, 0)
    greet(col, 2 * y + 1 - core)
    for dy in range(1, 4):
        greet(col, 2 * ((y + dy) % 4) + core)

    def greet_column(s, _):
        source = (64 * (col % 6) + 8 * s + row) // per
        source_row = col // 6

        @pl.when(jnp.logical_not(jnp.logical_and(source == col, source_row == row)))
        def _():
            greet(source, source_row)
        return 0

    lax.fori_loop(0, 8, greet_column, 0)
    expected = jnp.int32(COLS - 1 + 4)
    for t in range(per):
        expected = expected + jnp.where(column_sends(t), 1, 0)
    z_out[...] = jnp.zeros_like(z_out)
    for load in loads:
        load.wait()
    gather.stage(panel)
    pl.semaphore_wait(barrier, expected)

    def pivot_z(dz):
        target = ((zi + dz) % ZS) * XS + xi
        return remote(pivot.at[core], full.at[zi, xi, core], zs_send, zs_recv.at[zi], target, row)

    def pivot_from(z):
        part = full.at[z, xi, core]
        return local(part, part, zs_recv.at[z])

    def pivot_x(part, dx):
        rows = full.at[pl.ds(0, 2), xi, core] if part == 0 else full.at[pl.ds(2, ZS - 2), xi, core]
        return remote(rows, rows, zx_send.at[part, dx - 1], zx_recv.at[part, dx - 1],
                      zi * XS + (xi + dx) % XS, row)

    def exchange(part):
        rows = full.at[pl.ds(0, 2), :, core] if part == 0 else full.at[pl.ds(2, ZS - 2), :, core]
        return remote(rows, rows, ex_send.at[part], ex_recv.at[part], col, 2 * y + 1 - core)

    local(pivot.at[core], full.at[zi, xi, core], zs_recv.at[zi]).start()
    for dz in (4, 3, 5, 2, 6, 1, 7):
        pivot_z(dz).start()
    gather.spread()

    def send_column(t, _):
        slot, target_col, target_row, own = column_target(t)
        there = mc.at[slot, target_row]

        @pl.when(column_sends(t))
        def _():
            remote(staged.at[t], there, c_send, c_recv, target_col, target_row).start()

        @pl.when(own)
        def _():
            local(staged.at[t], there, c_recv).start()
        return 0

    lax.fori_loop(0, per, send_column, 0)
    where = slots_of(fill, blocks * row, 0, SLOTS, halves)
    for z in range(2):
        pivot_from(z).wait()
    for dx in range(1, XS):
        pivot_x(0, dx).start()
    for z in range(2, ZS):
        pivot_from(z).wait()
    for dx in range(1, XS):
        pivot_x(1, dx).start()
    gather.pack(where)
    for dx in range(1, XS):
        pivot_x(0, dx).wait_recv()
    exchange(0).start()
    def pivot_rest():
        for dx in range(1, XS):
            pivot_x(1, dx).wait_recv()
        exchange(1).start()

    def column_y(dy):
        part = mc.at[:, row]
        return remote(part, part, y_send.at[dy - 1], y_recv.at[dy - 1], col, 2 * ((y + dy) % 4) + core)

    def column_first():
        part = mc.at[:, row]
        local(part, part, c_recv).wait()
        for dy in range(1, 4):
            column_y(dy).start()

    def column_core(i):
        part = mc.at[:, 2 * i + core]
        return remote(part, part, k_send.at[i], k_recv.at[i], col, 2 * y + 1 - core)

    def column_next():
        for dy in range(1, 4):
            column_y(dy).wait_recv()
        for i in range(4):
            column_core(i).start()

    plan = {
        (0, 3): pivot_rest,
        (0, 8): gather.first,
        (0, 14): column_first,
        (1, 8): functools.partial(gather.next, 1),
        (2, 6): functools.partial(gather.next, 2),
        (2, 10): column_next,
        (3, 4): functools.partial(gather.next, 3),
    }

    n = z_out.shape[0]
    exchange(0).wait_recv()
    for k in range(n // TILE):
        lo, hi = k * TILE, (k + 1) * TILE
        if k == 0:
            groups = [full[g // 8, (g // 2) % 4, g % 2, :, lo:hi] for g in range(TILE // 8)]
        else:
            groups = [work[lo + 8 * g : lo + 8 * g + 8, lo:hi] for g in range(TILE // 8)]

        def hook(g, k=k):
            if (k, g) in plan:
                plan[k, g]()

        rows = invert_tile(groups, hook)
        for g in range(TILE // 8):
            z_out[lo + 8 * g : lo + 8 * g + 8, lo:hi] = rows[g]
        zk = z_out[lo:hi, lo:hi]
        if k > 0:
            z_out[lo:hi, :lo] = mm(zk, z_out[lo:hi, :lo], NN)
        if hi < n:
            if k == 0:
                exchange(1).wait_recv()
                below = full[2:].reshape(n - hi, n)
            else:
                below = work[hi:, :]
            p = mm(below[:, lo:hi], zk, NT)
            work[hi:, hi:] = below[:, hi:] - mm(p, p, NT)
            z_out[hi:, :hi] = z_out[hi:, :hi] - mm(p, z_out[lo:hi, :hi], NN)

    for i in range(4):
        column_core(i).wait_recv()

    def flag(block, h):
        return jnp.where(fill[h, block] != 0, 1.0, 0.0).astype(F32)

    rows = []
    for i in range(2):
        part = mc[4 * i : 4 * i + 4]
        rows.append(jnp.concatenate(
            [part[:, :, h].reshape(B, B) * flag(2 * col + i, h) for h in range(2)], axis=1))
    zs = split(z_out[...])
    xc = mm3(zs, split(jnp.concatenate(rows, axis=0)), NT)
    t_hi[...], t_lo[...] = split(mm3(zs, split(xc), TN))

    gather.last()
    for i in range(4):
        column_core(i).wait_send()
    for dy in range(1, 4):
        column_y(dy).wait_send()
    for part in range(2):
        exchange(part).wait_send()
        for dx in range(1, XS):
            pivot_x(part, dx).wait_send()
    local(full.at[pl.ds(0, ZS - 1), 0, core], full.at[pl.ds(0, ZS - 1), 0, core], zs_send).wait()

    def sent_column(t, _):
        @pl.when(column_sends(t))
        def _():
            local(staged.at[0], staged.at[0], c_send).wait()
        return 0

    lax.fori_loop(0, per, sent_column, 0)


def gather_and_factor(fill, pivot, panel):
    n = panel.shape[1]
    per = panel.shape[0] // 8
    dma = pltpu.SemaphoreType.DMA
    vmem = pl.BlockSpec(memory_space=pltpu.VMEM)
    anywhere = pl.BlockSpec(memory_space=pl.ANY)
    return pl.pallas_call(
        gather_kernel,
        out_shape=(
            jax.ShapeDtypeStruct((n, n), F32),
            jax.ShapeDtypeStruct((n, n), BF16),
            jax.ShapeDtypeStruct((n, n), BF16),
            jax.ShapeDtypeStruct((SLOTS, ZS, XS, 8, B), F32),
        ),
        in_specs=[pl.BlockSpec(memory_space=pltpu.HBM)] * 3,
        out_specs=(vmem, vmem, vmem, anywhere),
        scratch_shapes=[
            pltpu.SMEM(fill.shape, jnp.int32),
            pltpu.VMEM((2, 8, n), F32),
            pltpu.VMEM(panel.shape, F32),
            pltpu.VMEM((n, n), F32),
            pltpu.VMEM((ZS, XS, 2, 8, n), F32),
            pltpu.VMEM((8, ROWS, 2, 8, B), F32),
            dma((3,)), dma, dma((ZS,)), dma((2, 3)), dma((2, 3)), dma((2,)), dma((2,)), dma, dma,
            dma((3,)), dma((3,)), dma((4,)), dma((4,)),
        ] + slab_scratch(per, SLOTS),
        compiler_params=pltpu.CompilerParams(
            has_side_effects=True, collective_id=0, vmem_limit_bytes=30 << 20),
        cost_estimate=pl.CostEstimate(flops=40_000_000_000, bytes_accessed=60_000_000, transcendentals=0),
        name="gather_and_factor",
    )(fill, pivot.reshape(2, 8, n), panel)


def gather_more_kernel(first, fill, panel, slab, staged, queued, packed, *sems):
    row = lax.axis_index("row")
    halves = queued.shape[0]
    gather = SlabGather(staged, queued, packed, slab, *sems)
    gather.stage(panel)
    gather.spread()
    gather.pack(slots_of(fill, halves // 2 * row, first[0], SLOTS, halves))
    gather.first()
    for step in range(1, 4):
        gather.next(step)
    gather.last()


def gather_more(first, fill, panel):
    per = panel.shape[0] // 8
    smem = pl.BlockSpec(memory_space=pltpu.SMEM)
    return pl.pallas_call(
        gather_more_kernel,
        out_shape=jax.ShapeDtypeStruct((SLOTS, ZS, XS, 8, B), F32),
        in_specs=[smem, smem, pl.BlockSpec(memory_space=pltpu.VMEM)],
        out_specs=pl.BlockSpec(memory_space=pl.ANY),
        scratch_shapes=slab_scratch(per, SLOTS),
        compiler_params=pltpu.CompilerParams(has_side_effects=True, vmem_limit_bytes=60 << 20),
        name="gather_more",
    )(first, fill, panel)


def add_blocks(fill, base, first, t_hi, t_lo, slab, blocks, before, after):
    seen = jnp.int32(0)
    for b in range(blocks.shape[0]):
        before(b)
        for h in range(2):
            on = fill[h, base + b] != 0
            slot = seen - first

            @pl.when(jnp.logical_and(on, jnp.logical_and(slot >= 0, slot < SLOTS)))
            def _(b=b, h=h, slot=slot):
                m = split(jnp.concatenate([slab[slot, :, x].reshape(8 * ZS, B) for x in range(XS)], axis=0))
                t = (t_hi[B * h : B * h + B], t_lo[B * h : B * h + B])
                blocks[b] = blocks[b] - mm3(m, t, NN)

            seen = seen + jnp.where(on, 1, 0)
        after(b)


def update_kernel(fill_any, z, t_hi, t_lo, slab, panel, held, updated, own, most,
                  fill, blocks, in_sem, write_sem):
    col, row = lax.axis_index("col"), lax.axis_index("row")
    count = blocks.shape[0]
    base = count * row
    get_fill = local(fill_any, fill, in_sem)
    get_fill.start()
    get_fill.wait()

    def touched(b):
        return jnp.logical_or(fill[0, base + b] != 0, fill[1, base + b] != 0)

    def write(b):
        return local(blocks.at[b], updated.at[pl.ds(B * b, B)], write_sem.at[b])

    def keep(b):
        return local(held.at[pl.ds(B * b, B)], updated.at[pl.ds(B * b, B)], write_sem.at[b])

    for b in range(count):
        @pl.when(jnp.logical_not(touched(b)))
        def _(b=b):
            keep(b).start()

    top = jnp.int32(0)
    for r in range(ROWS):
        total = jnp.int32(0)
        for b in range(count):
            for h in range(2):
                total = total + jnp.where(fill[h, count * r + b] != 0, 1, 0)
        top = jnp.maximum(top, total)
    most[0] = top

    masked = []
    for t in range(panel.shape[0] // 8):
        block = base + (panel.shape[0] * col + 8 * t) // B
        masked.append(jnp.concatenate(
            [panel[8 * t : 8 * t + 8, B * h : B * h + B]
             * jnp.where(fill[h, block] != 0, 1.0, 0.0).astype(F32) for h in range(2)], axis=1))
    own[...] = mm(jnp.concatenate(masked, axis=0), z[...], NT)

    def before(b):
        @pl.when(touched(b))
        def _():
            blocks[b] = held[B * b : B * b + B]

    def after(b):
        @pl.when(touched(b))
        def _():
            write(b).start()

    add_blocks(fill, base, 0, t_hi, t_lo, slab, blocks, before, after)
    for b in range(count):
        write(b).wait()


def apply_update(fill, z, t_hi, t_lo, slab, panel, held):
    count = held.shape[0] // B
    width = held.shape[1]
    dma = pltpu.SemaphoreType.DMA
    vmem = pl.BlockSpec(memory_space=pltpu.VMEM)
    hbm = pl.BlockSpec(memory_space=pltpu.HBM)
    smem = pl.BlockSpec(memory_space=pltpu.SMEM)
    return pl.pallas_call(
        update_kernel,
        out_shape=(
            jax.ShapeDtypeStruct(held.shape, F32),
            jax.ShapeDtypeStruct(panel.shape, F32),
            jax.ShapeDtypeStruct((1,), jnp.int32),
        ),
        in_specs=[hbm, vmem, vmem, vmem, vmem, vmem, vmem],
        out_specs=(hbm, vmem, smem),
        scratch_shapes=[
            pltpu.SMEM(fill.shape, jnp.int32),
            pltpu.VMEM((count, B, width), F32),
            dma, dma((count,)),
        ],
        compiler_params=pltpu.CompilerParams(vmem_limit_bytes=30 << 20),
        name="apply_update",
    )(fill, z, t_hi, t_lo, slab, panel, held)


def update_more_kernel(first, fill, t_hi, t_lo, slab, before_any, after_any, blocks, read_sem, write_sem):
    count = blocks.shape[0]
    base = count * lax.axis_index("row")

    def read(b):
        return local(before_any.at[pl.ds(B * b, B)], blocks.at[b], read_sem.at[b])

    def write(b):
        return local(blocks.at[b], after_any.at[pl.ds(B * b, B)], write_sem.at[b])

    for b in range(count):
        read(b).start()
    add_blocks(fill, base, first[0], t_hi, t_lo, slab, blocks,
               lambda b: read(b).wait(), lambda b: write(b).start())
    for b in range(count):
        write(b).wait()


def update_more(first, fill, t_hi, t_lo, slab, updated):
    count = updated.shape[0] // B
    dma = pltpu.SemaphoreType.DMA
    vmem = pl.BlockSpec(memory_space=pltpu.VMEM)
    hbm = pl.BlockSpec(memory_space=pltpu.HBM)
    smem = pl.BlockSpec(memory_space=pltpu.SMEM)
    return pl.pallas_call(
        update_more_kernel,
        out_shape=jax.ShapeDtypeStruct(updated.shape, F32),
        in_specs=[smem, smem, vmem, vmem, vmem, hbm],
        out_specs=hbm,
        scratch_shapes=[
            pltpu.VMEM((count, B, updated.shape[1]), F32), dma((count,)), dma((count,))],
        input_output_aliases={5: 0},
        compiler_params=pltpu.CompilerParams(vmem_limit_bytes=60 << 20),
        name="update_more",
    )(first, fill, t_hi, t_lo, slab, updated)


def per_device(trailing, panel_rows, pivot_block, panel_fill):
    fill = panel_fill.T
    z, t_hi, t_lo, slab = gather_and_factor(fill, pivot_block, panel_rows)
    updated, own, most = apply_update(fill, z, t_hi, t_lo, slab, panel_rows, trailing)

    def body(state):
        first, updated = state
        more = gather_more(first, fill, panel_rows)
        return first + SLOTS, update_more(first, fill, t_hi, t_lo, more, updated)

    start = jnp.full((1,), SLOTS, jnp.int32)
    _, updated = lax.while_loop(lambda state: state[0][0] < most[0], body, (start, updated))
    return updated, own


def solution(mesh):
    in_specs = (P("row", "col"), P(("row", "col"), None), P("col", None), P())
    out_specs = (P("row", "col"), P(("row", "col"), None))
    return jax.shard_map(
        per_device, mesh=mesh, in_specs=in_specs, out_specs=out_specs, check_vma=False
    )
```

```python
import functools

import jax
import jax.numpy as jnp
from jax import lax
from jax.experimental import pallas as pl
from jax.experimental.pallas import tpu as pltpu
from jax.sharding import PartitionSpec as P

F32 = jnp.float32
BF16 = jnp.bfloat16
HIGHEST = lax.Precision.HIGHEST
NT = (((1,), (1,)), ((), ()))
NN = (((1,), (0,)), ((), ()))
TN = (((0,), (0,)), ((), ()))

ZS, XS = 8, 4
COLS, ROWS = ZS * XS, 8
B = 256
TILE = 128


def mm(a, b, dims):
    return lax.dot_general(a, b, dims, precision=HIGHEST, preferred_element_type=F32)


def split(v):
    hi = v.astype(BF16)
    return hi, (v - hi.astype(F32)).astype(BF16)


def mm3(a, b, dims):
    dot = functools.partial(lax.dot_general, dimension_numbers=dims, preferred_element_type=F32)
    return dot(a[0], b[0]) + (dot(a[0], b[1]) + dot(a[1], b[0]))


def spread_row(v, r):
    return jnp.broadcast_to(v[r : r + 1, :], v.shape)


def invert_tile(groups, hook):
    n = groups[0].shape[1]
    count = n // 8
    lane = lax.broadcasted_iota(jnp.int32, (8, n), 1)
    sub = lax.broadcasted_iota(jnp.int32, (8, n), 0)
    left = list(groups)
    right = [jnp.where(lane == sub + 8 * g, 1.0, 0.0).astype(F32) for g in range(count)]
    done = []

    def columns(h, g):
        return [
            jnp.broadcast_to(left[h][:, 8 * g + r : 8 * g + r + 1], (8, n)) for r in range(8)
        ]

    def total(terms):
        while len(terms) > 1:
            terms = [a + b for a, b in zip(terms[::2], terms[1::2])]
        return terms[0]

    for g in range(count):
        hook(g)
        pivot = columns(g, g)
        below = {h: columns(h, g) for h in range(g + 1, count)}
        wide, inv = left[g], right[g]
        final = inv
        raw, raw_wide, raw_inv = list(pivot), wide, inv
        for r in range(0, 8, 2):
            a, b, d = (
                spread_row(raw[r], r),
                spread_row(raw[r + 1], r),
                spread_row(raw[r + 1], r + 1),
            )
            det = a * d - b * b
            scale = 1.0 / det
            an, bn, dn = a * scale, b * scale, d * scale
            m0, m1 = pivot[r], pivot[r + 1]
            e0, e1 = spread_row(raw_inv, r), spread_row(raw_inv, r + 1)
            over_a = 1.0 / a
            f0 = e0 * lax.rsqrt(a)
            f1 = (e1 - (b * over_a) * e0) * lax.rsqrt(det * over_a)
            final = jnp.where(sub == r, f0, jnp.where(sub == r + 1, f1, final))

            def step(w, ahead):
                w0, w1 = spread_row(ahead, r), spread_row(ahead, r + 1)
                y0 = dn * w0 - bn * w1
                y1 = an * w1 - bn * w0
                rest = w - (m0 * y0 + m1 * y1)
                return jnp.where(sub == r, y0, jnp.where(sub == r + 1, y1, rest)), rest

            for q in range(r + 2, 8):
                pivot[q], raw[q] = step(pivot[q], raw[q])
            wide, raw_wide = step(wide, raw_wide)
            inv, raw_inv = step(inv, raw_inv)
        done.append(final)
        wide_rows = [spread_row(wide, r) for r in range(8)]
        inv_rows = [spread_row(inv, r) for r in range(8)]
        for h in range(g + 1, count):
            left[h] = left[h] - total([below[h][r] * wide_rows[r] for r in range(8)])
            right[h] = right[h] - total([below[h][r] * inv_rows[r] for r in range(8)])
    return done

SLOTS = 8


def remote(src, dst, send, recv, col, row):
    return pltpu.make_async_remote_copy(
        src_ref=src, dst_ref=dst, send_sem=send, recv_sem=recv,
        device_id={"col": col, "row": row}, device_id_type=pl.DeviceIdType.MESH)


local = pltpu.make_async_copy


def place():
    col, row = lax.axis_index("col"), lax.axis_index("row")
    return col, row, col // XS, col % XS, row // 2, row % 2


def slots_of(fill, base, first, slots, halves):
    where = [jnp.int32(0)] * slots
    seen = jnp.int32(0)
    for n in range(halves):
        on = fill[n % 2, base + n // 2] != 0
        for k in range(slots):
            hit = jnp.logical_and(on, seen == first + k)
            where[k] = jnp.where(hit, n, where[k])
        seen = seen + jnp.where(on, 1, 0)
    return where


class SlabGather:
    def __init__(self, staged, queued, packed, slab, q_send, q_recv, x_send, x_recv, x_own, r_send, r_recv):
        self.refs = staged, queued, packed, slab
        self.q_send, self.q_recv, self.x_own = q_send, q_recv, x_own
        self.x_send, self.x_recv, self.r_send, self.r_recv = x_send, x_recv, r_send, r_recv
        self.slots = packed.shape[0]
        self.per = staged.shape[0]

    def stage(self, panel):
        staged = self.refs[0]
        for t in range(self.per):
            for h in range(2):
                staged[t, h] = panel[8 * t : 8 * t + 8, B * h : B * h + B]

    def target(self, t):
        index = self.per * place()[0] + t
        return index // COLS, (index % ZS) * XS + (index % COLS) // ZS

    def spread(self):
        staged, queued, _, _ = self.refs
        col, row, *_ = place()

        def send(t, _):
            block, target = self.target(t)
            there = queued.at[pl.ds(2 * block, 2)]

            @pl.when(target != col)
            def _():
                remote(staged.at[t], there, self.q_send, self.q_recv, target, row).start()

            @pl.when(target == col)
            def _():
                local(staged.at[t], there, self.q_recv).start()
            return 0

        lax.fori_loop(0, self.per, send, 0)

    def along_x(self, dx):
        _, _, packed, slab = self.refs
        col, row, zi, xi, *_ = place()
        half = self.slots // 2
        return remote(packed.at[pl.ds(0, half)], slab.at[pl.ds(0, half), zi, xi],
                      self.x_send.at[dx - 1], self.x_recv.at[dx - 1], zi * XS + (xi + dx) % XS, row)

    def across_x(self, z, start, count, dx):
        slab = self.refs[3]
        col, row, zi, xi, *_ = place()
        part = slab.at[pl.ds(start, count), z, xi]
        return remote(part, part, self.x_send.at[dx + 2], self.x_recv.at[dx + 2],
                      zi * XS + (xi + dx) % XS, row)

    def pass_across(self, z):
        half = self.slots // 2
        for dx in range(1, XS):
            self.across_x(z, half, half, dx).start()

    def own(self):
        _, _, packed, slab = self.refs
        _, _, zi, xi, *_ = place()
        return local(packed, slab.at[:, zi, xi], self.x_own)

    def pack(self, where):
        _, queued, packed, _ = self.refs
        zi = place()[2]
        local(queued, queued, self.q_recv).wait()
        for k in range(self.slots):
            packed[k] = queued[where[k]]
        self.own().start()
        for dx in range(1, XS):
            self.along_x(dx).start()
        self.own().wait()
        for side in range(2):
            self.ring(1, 0, side).start()
        self.pass_across(zi)

    def source(self, step, side):
        sign = 1 if side == 0 else -1
        return (place()[2] - sign * step + ZS) % ZS

    def ring(self, kind, step, side):
        slab = self.refs[3]
        col, row, zi, xi, *_ = place()
        sign = 1 if side == 0 else -1
        half = self.slots // 2
        rows = pl.ds(kind * half, half) if step < 3 else pl.ds(kind * half + side * (half // 2), half // 2)
        part = slab.at[rows, self.source(step, side)] if kind == 0 else slab.at[rows, self.source(step, side), xi]
        target = ((zi + sign + ZS) % ZS) * XS + xi
        return remote(part, part, self.r_send.at[kind, side, step], self.r_recv.at[kind, side, step], target, row)

    def first(self):
        for dx in range(1, XS):
            self.along_x(dx).wait_recv()
        for side in range(2):
            self.ring(0, 0, side).start()
        self.next_across(1)

    def next_across(self, step):
        for side in range(2):
            self.ring(1, step - 1, side).wait_recv()
            if step < 4:
                self.ring(1, step, side).start()
        if step < 4:
            for side in range(2):
                self.pass_across(self.source(step, side))
        else:
            self.pass_across(self.source(4, 0))

    def next(self, step):
        for side in range(2):
            self.ring(0, step - 1, side).wait_recv()
            self.ring(0, step, side).start()
        self.next_across(step + 1)

    def last(self):
        staged, _, _, slab = self.refs
        half = self.slots // 2
        col = place()[0]
        for side in range(2):
            self.ring(0, 3, side).wait_recv()
        line = slab.at[pl.ds(half, half), :, 0]
        for dx in range(1, XS):
            local(line, line, self.x_recv.at[dx + 2]).wait()
            local(line, line, self.x_send.at[dx + 2]).wait()
            self.along_x(dx).wait_send()
        for kind in range(2):
            for side in range(2):
                for step in range(4):
                    self.ring(kind, step, side).wait_send()

        def sent(t, _):
            @pl.when(self.target(t)[1] != col)
            def _():
                local(staged.at[0], staged.at[0], self.q_send).wait()
            return 0

        lax.fori_loop(0, self.per, sent, 0)


def slab_scratch(per, slots):
    dma = pltpu.SemaphoreType.DMA
    return [
        pltpu.VMEM((per, 2, 8, B), F32), pltpu.VMEM((2 * per, 8, B), F32), pltpu.VMEM((slots, 8, B), F32),
        dma, dma, dma((6,)), dma((6,)), dma, dma((2, 2, 4)), dma((2, 2, 4)),
    ]


def gather_kernel(fill_any, pivot_any, panel_any, z_out, t_hi, t_lo, slab, fill, pivot, panel, work, full, mc,
                  in_sem, zs_send, zs_recv, zx_send, zx_recv, ex_send, ex_recv, c_send, c_recv,
                  y_send, y_recv, k_send, k_recv, staged, queued, packed, *slab_sems):
    col, row, zi, xi, y, core = place()
    halves = queued.shape[0]
    per = staged.shape[0]
    blocks = halves // 2
    gather = SlabGather(staged, queued, packed, slab, *slab_sems)
    loads = [
        local(fill_any, fill, in_sem.at[0]),
        local(pivot_any, pivot, in_sem.at[1]),
        local(panel_any, panel, in_sem.at[2]),
    ]
    for load in loads:
        load.start()

    def column_target(t):
        index = per * col + t
        target_col, target_row = 6 * row + index // 64, index % 8
        own = jnp.logical_and(target_col == col, target_row == row)
        return (index % 64) // 8, target_col, target_row, own

    def column_sends(t):
        _, target_col, _, own = column_target(t)
        return jnp.logical_and(target_col < COLS, jnp.logical_not(own))

    barrier = pltpu.get_barrier_semaphore()

    def greet(c, r):
        pl.semaphore_signal(barrier, inc=1, device_id={"col": c, "row": r}, device_id_type=pl.DeviceIdType.MESH)

    def greet_slab(i, _):
        greet((col + i) % COLS, row)
        return 0

    lax.fori_loop(1, COLS, greet_slab, 0)
    greet(col, 2 * y + 1 - core)
    for dy in range(1, 4):
        greet(col, 2 * ((y + dy) % 4) + core)

    def greet_column(s, _):
        source = (64 * (col % 6) + 8 * s + row) // per
        source_row = col // 6

        @pl.when(jnp.logical_not(jnp.logical_and(source == col, source_row == row)))
        def _():
            greet(source, source_row)
        return 0

    lax.fori_loop(0, 8, greet_column, 0)
    expected = jnp.int32(COLS - 1 + 4)
    for t in range(per):
        expected = expected + jnp.where(column_sends(t), 1, 0)
    z_out[...] = jnp.zeros_like(z_out)
    for load in loads:
        load.wait()
    gather.stage(panel)
    pl.semaphore_wait(barrier, expected)

    def pivot_z(dz):
        target = ((zi + dz) % ZS) * XS + xi
        return remote(pivot.at[core], full.at[zi, xi, core], zs_send, zs_recv.at[zi], target, row)

    def pivot_from(z):
        part = full.at[z, xi, core]
        return local(part, part, zs_recv.at[z])

    def pivot_x(part, dx):
        rows = full.at[pl.ds(0, 2), xi, core] if part == 0 else full.at[pl.ds(2, ZS - 2), xi, core]
        return remote(rows, rows, zx_send.at[part, dx - 1], zx_recv.at[part, dx - 1],
                      zi * XS + (xi + dx) % XS, row)

    def exchange(part):
        rows = full.at[pl.ds(0, 2), :, core] if part == 0 else full.at[pl.ds(2, ZS - 2), :, core]
        return remote(rows, rows, ex_send.at[part], ex_recv.at[part], col, 2 * y + 1 - core)

    local(pivot.at[core], full.at[zi, xi, core], zs_recv.at[zi]).start()
    for dz in (4, 3, 5, 2, 6, 1, 7):
        pivot_z(dz).start()
    gather.spread()

    def send_column(t, _):
        slot, target_col, target_row, own = column_target(t)
        there = mc.at[slot, target_row]

        @pl.when(column_sends(t))
        def _():
            remote(staged.at[t], there, c_send, c_recv, target_col, target_row).start()

        @pl.when(own)
        def _():
            local(staged.at[t], there, c_recv).start()
        return 0

    lax.fori_loop(0, per, send_column, 0)
    where = slots_of(fill, blocks * row, 0, SLOTS, halves)
    for z in range(2):
        pivot_from(z).wait()
    for dx in range(1, XS):
        pivot_x(0, dx).start()
    for z in range(2, ZS):
        pivot_from(z).wait()
    for dx in range(1, XS):
        pivot_x(1, dx).start()
    gather.pack(where)
    for dx in range(1, XS):
        pivot_x(0, dx).wait_recv()
    exchange(0).start()
    def pivot_rest():
        for dx in range(1, XS):
            pivot_x(1, dx).wait_recv()
        exchange(1).start()

    def column_y(dy):
        part = mc.at[:, row]
        return remote(part, part, y_send.at[dy - 1], y_recv.at[dy - 1], col, 2 * ((y + dy) % 4) + core)

    def column_first():
        part = mc.at[:, row]
        local(part, part, c_recv).wait()
        for dy in range(1, 4):
            column_y(dy).start()

    def column_core(i):
        part = mc.at[:, 2 * i + core]
        return remote(part, part, k_send.at[i], k_recv.at[i], col, 2 * y + 1 - core)

    def column_next():
        for dy in range(1, 4):
            column_y(dy).wait_recv()
        for i in range(4):
            column_core(i).start()

    plan = {
        (0, 3): pivot_rest,
        (0, 8): gather.first,
        (0, 14): column_first,
        (1, 8): functools.partial(gather.next, 1),
        (2, 6): functools.partial(gather.next, 2),
        (2, 10): column_next,
        (3, 4): functools.partial(gather.next, 3),
    }

    n = z_out.shape[0]
    exchange(0).wait_recv()
    for k in range(n // TILE):
        lo, hi = k * TILE, (k + 1) * TILE
        if k == 0:
            groups = [full[g // 8, (g // 2) % 4, g % 2, :, lo:hi] for g in range(TILE // 8)]
        else:
            groups = [work[lo + 8 * g : lo + 8 * g + 8, lo:hi] for g in range(TILE // 8)]

        def hook(g, k=k):
            if (k, g) in plan:
                plan[k, g]()

        rows = invert_tile(groups, hook)
        for g in range(TILE // 8):
            z_out[lo + 8 * g : lo + 8 * g + 8, lo:hi] = rows[g]
        zk = z_out[lo:hi, lo:hi]
        if k > 0:
            z_out[lo:hi, :lo] = mm(zk, z_out[lo:hi, :lo], NN)
        if hi < n:
            if k == 0:
                exchange(1).wait_recv()
                below = full[2:].reshape(n - hi, n)
            else:
                below = work[hi:, :]
            p = mm(below[:, lo:hi], zk, NT)
            work[hi:, hi:] = below[:, hi:] - mm(p, p, NT)
            z_out[hi:, :hi] = z_out[hi:, :hi] - mm(p, z_out[lo:hi, :hi], NN)

    for i in range(4):
        column_core(i).wait_recv()

    def flag(block, h):
        return jnp.where(fill[h, block] != 0, 1.0, 0.0).astype(F32)

    rows = []
    for i in range(2):
        part = mc[4 * i : 4 * i + 4]
        rows.append(jnp.concatenate(
            [part[:, :, h].reshape(B, B) * flag(2 * col + i, h) for h in range(2)], axis=1))
    zs = split(z_out[...])
    xc = mm3(zs, split(jnp.concatenate(rows, axis=0)), NT)
    t_hi[...], t_lo[...] = split(mm3(zs, split(xc), TN))

    gather.last()
    for i in range(4):
        column_core(i).wait_send()
    for dy in range(1, 4):
        column_y(dy).wait_send()
    for part in range(2):
        exchange(part).wait_send()
        for dx in range(1, XS):
            pivot_x(part, dx).wait_send()
    local(full.at[pl.ds(0, ZS - 1), 0, core], full.at[pl.ds(0, ZS - 1), 0, core], zs_send).wait()

    def sent_column(t, _):
        @pl.when(column_sends(t))
        def _():
            local(staged.at[0], staged.at[0], c_send).wait()
        return 0

    lax.fori_loop(0, per, sent_column, 0)


def gather_and_factor(fill, pivot, panel):
    n = panel.shape[1]
    per = panel.shape[0] // 8
    dma = pltpu.SemaphoreType.DMA
    vmem = pl.BlockSpec(memory_space=pltpu.VMEM)
    anywhere = pl.BlockSpec(memory_space=pl.ANY)
    return pl.pallas_call(
        gather_kernel,
        out_shape=(
            jax.ShapeDtypeStruct((n, n), F32),
            jax.ShapeDtypeStruct((n, n), BF16),
            jax.ShapeDtypeStruct((n, n), BF16),
            jax.ShapeDtypeStruct((SLOTS, ZS, XS, 8, B), F32),
        ),
        in_specs=[pl.BlockSpec(memory_space=pltpu.HBM)] * 3,
        out_specs=(vmem, vmem, vmem, anywhere),
        scratch_shapes=[
            pltpu.SMEM(fill.shape, jnp.int32),
            pltpu.VMEM((2, 8, n), F32),
            pltpu.VMEM(panel.shape, F32),
            pltpu.VMEM((n, n), F32),
            pltpu.VMEM((ZS, XS, 2, 8, n), F32),
            pltpu.VMEM((8, ROWS, 2, 8, B), F32),
            dma((3,)), dma, dma((ZS,)), dma((2, 3)), dma((2, 3)), dma((2,)), dma((2,)), dma, dma,
            dma((3,)), dma((3,)), dma((4,)), dma((4,)),
        ] + slab_scratch(per, SLOTS),
        compiler_params=pltpu.CompilerParams(
            has_side_effects=True, collective_id=0, vmem_limit_bytes=30 << 20),
        cost_estimate=pl.CostEstimate(flops=40_000_000_000, bytes_accessed=60_000_000, transcendentals=0),
        name="gather_and_factor",
    )(fill, pivot.reshape(2, 8, n), panel)


def gather_more_kernel(first, fill, panel, slab, staged, queued, packed, *sems):
    row = lax.axis_index("row")
    halves = queued.shape[0]
    gather = SlabGather(staged, queued, packed, slab, *sems)
    gather.stage(panel)
    gather.spread()
    gather.pack(slots_of(fill, halves // 2 * row, first[0], SLOTS, halves))
    gather.first()
    for step in range(1, 4):
        gather.next(step)
    gather.last()


def gather_more(first, fill, panel):
    per = panel.shape[0] // 8
    smem = pl.BlockSpec(memory_space=pltpu.SMEM)
    return pl.pallas_call(
        gather_more_kernel,
        out_shape=jax.ShapeDtypeStruct((SLOTS, ZS, XS, 8, B), F32),
        in_specs=[smem, smem, pl.BlockSpec(memory_space=pltpu.VMEM)],
        out_specs=pl.BlockSpec(memory_space=pl.ANY),
        scratch_shapes=slab_scratch(per, SLOTS),
        compiler_params=pltpu.CompilerParams(has_side_effects=True, vmem_limit_bytes=60 << 20),
        name="gather_more",
    )(first, fill, panel)


def add_blocks(fill, base, first, t_hi, t_lo, slab, blocks, before, after):
    seen = jnp.int32(0)
    for b in range(blocks.shape[0]):
        before(b)
        for h in range(2):
            on = fill[h, base + b] != 0
            slot = seen - first

            @pl.when(jnp.logical_and(on, jnp.logical_and(slot >= 0, slot < SLOTS)))
            def _(b=b, h=h, slot=slot):
                m = split(jnp.concatenate([slab[slot, :, x].reshape(8 * ZS, B) for x in range(XS)], axis=0))
                t = (t_hi[B * h : B * h + B], t_lo[B * h : B * h + B])
                blocks[b] = blocks[b] - mm3(m, t, NN)

            seen = seen + jnp.where(on, 1, 0)
        after(b)


def update_kernel(fill_any, z, t_hi, t_lo, slab, panel, held, updated, own, most,
                  fill, blocks, in_sem, write_sem):
    col, row = lax.axis_index("col"), lax.axis_index("row")
    count = blocks.shape[0]
    base = count * row
    get_fill = local(fill_any, fill, in_sem)
    get_fill.start()
    get_fill.wait()

    def touched(b):
        return jnp.logical_or(fill[0, base + b] != 0, fill[1, base + b] != 0)

    def write(b):
        return local(blocks.at[b], updated.at[pl.ds(B * b, B)], write_sem.at[b])

    def keep(b):
        return local(held.at[pl.ds(B * b, B)], updated.at[pl.ds(B * b, B)], write_sem.at[b])

    for b in range(count):
        @pl.when(jnp.logical_not(touched(b)))
        def _(b=b):
            keep(b).start()

    top = jnp.int32(0)
    for r in range(ROWS):
        total = jnp.int32(0)
        for b in range(count):
            for h in range(2):
                total = total + jnp.where(fill[h, count * r + b] != 0, 1, 0)
        top = jnp.maximum(top, total)
    most[0] = top

    masked = []
    for t in range(panel.shape[0] // 8):
        block = base + (panel.shape[0] * col + 8 * t) // B
        masked.append(jnp.concatenate(
            [panel[8 * t : 8 * t + 8, B * h : B * h + B]
             * jnp.where(fill[h, block] != 0, 1.0, 0.0).astype(F32) for h in range(2)], axis=1))
    own[...] = mm(jnp.concatenate(masked, axis=0), z[...], NT)

    def before(b):
        @pl.when(touched(b))
        def _():
            blocks[b] = held[B * b : B * b + B]

    def after(b):
        @pl.when(touched(b))
        def _():
            write(b).start()

    add_blocks(fill, base, 0, t_hi, t_lo, slab, blocks, before, after)
    for b in range(count):
        write(b).wait()


def apply_update(fill, z, t_hi, t_lo, slab, panel, held):
    count = held.shape[0] // B
    width = held.shape[1]
    dma = pltpu.SemaphoreType.DMA
    vmem = pl.BlockSpec(memory_space=pltpu.VMEM)
    hbm = pl.BlockSpec(memory_space=pltpu.HBM)
    smem = pl.BlockSpec(memory_space=pltpu.SMEM)
    return pl.pallas_call(
        update_kernel,
        out_shape=(
            jax.ShapeDtypeStruct(held.shape, F32),
            jax.ShapeDtypeStruct(panel.shape, F32),
            jax.ShapeDtypeStruct((1,), jnp.int32),
        ),
        in_specs=[hbm, vmem, vmem, vmem, vmem, vmem, vmem],
        out_specs=(hbm, vmem, smem),
        scratch_shapes=[
            pltpu.SMEM(fill.shape, jnp.int32),
            pltpu.VMEM((count, B, width), F32),
            dma, dma((count,)),
        ],
        compiler_params=pltpu.CompilerParams(vmem_limit_bytes=30 << 20),
        name="apply_update",
    )(fill, z, t_hi, t_lo, slab, panel, held)


def update_more_kernel(first, fill, t_hi, t_lo, slab, before_any, after_any, blocks, read_sem, write_sem):
    count = blocks.shape[0]
    base = count * lax.axis_index("row")

    def read(b):
        return local(before_any.at[pl.ds(B * b, B)], blocks.at[b], read_sem.at[b])

    def write(b):
        return local(blocks.at[b], after_any.at[pl.ds(B * b, B)], write_sem.at[b])

    for b in range(count):
        read(b).start()
    add_blocks(fill, base, first[0], t_hi, t_lo, slab, blocks,
               lambda b: read(b).wait(), lambda b: write(b).start())
    for b in range(count):
        write(b).wait()


def update_more(first, fill, t_hi, t_lo, slab, updated):
    count = updated.shape[0] // B
    dma = pltpu.SemaphoreType.DMA
    vmem = pl.BlockSpec(memory_space=pltpu.VMEM)
    hbm = pl.BlockSpec(memory_space=pltpu.HBM)
    smem = pl.BlockSpec(memory_space=pltpu.SMEM)
    return pl.pallas_call(
        update_more_kernel,
        out_shape=jax.ShapeDtypeStruct(updated.shape, F32),
        in_specs=[smem, smem, vmem, vmem, vmem, hbm],
        out_specs=hbm,
        scratch_shapes=[
            pltpu.VMEM((count, B, updated.shape[1]), F32), dma((count,)), dma((count,))],
        input_output_aliases={5: 0},
        compiler_params=pltpu.CompilerParams(vmem_limit_bytes=60 << 20),
        name="update_more",
    )(first, fill, t_hi, t_lo, slab, updated)


def per_device(trailing, panel_rows, pivot_block, panel_fill):
    fill = panel_fill.T
    z, t_hi, t_lo, slab = gather_and_factor(fill, pivot_block, panel_rows)
    updated, own, most = apply_update(fill, z, t_hi, t_lo, slab, panel_rows, trailing)

    def body(state):
        first, updated = state
        more = gather_more(first, fill, panel_rows)
        return first + SLOTS, update_more(first, fill, t_hi, t_lo, more, updated)

    start = jnp.full((1,), SLOTS, jnp.int32)
    _, updated = lax.while_loop(lambda state: state[0][0] < most[0], body, (start, updated))
    return updated, own


def solution(mesh):
    in_specs = (P("row", "col"), P(("row", "col"), None), P("col", None), P())
    out_specs = (P("row", "col"), P(("row", "col"), None))
    return jax.shard_map(
        per_device, mesh=mesh, in_specs=in_specs, out_specs=out_specs, check_vma=False
    )
```
